32 devices in a mesh: grp: 2 (over y), chan: 4 (over z), tm: 2 (over x), head: 2 (over core).
Axes of the slice: x: 2, y: 2, z: 4, core: 2. Of those that a mesh axis runs over, the one named last changes fastest.
Arguments:
- strain: bfloat16 [128, 4096], P(('grp', 'tm', 'head'), 'chan'), parts along dimension 0, may hold values from -8 to 8, as said below
- stem_weight: bfloat16 [180, 1024], replicated, may hold values from -0.4375 to 0.4375
- attn_in: bfloat16 [1024, 3072], replicated, may hold values from -3 to 3
- attn_out: bfloat16 [1024, 1024], replicated, may hold values from -0.1875 to 0.1875
- pool_weight: bfloat16 [1024, 256], replicated, may hold values from -0.1875 to 0.1875
- neighbours: int32 [8, 6], P('grp'), parts along dimension 0, may hold values from -1 to 3, as said below
- seismo_embed: float32 [64, 256], P('grp'), parts along dimension 0, may hold values from -6 to 6
- colocated: int32 [64], P('grp'), parts along dimension 0, may hold values from 0 to 3
Outputs:
- encoded: bfloat16 [8, 512, 1024], P(('grp', 'tm', 'head'), 'chan'), parts along dimension 0
- seismic_loss: float32 [64], P('grp'), parts along dimension 0
The draws below stay inside these ranges and needn't reach their ends.
There are 2 independent parts, one for each index of `grp`. The reference program is written for one: setup_inputs(seed, part) draws one part's arguments, and reference() takes and returns one part's arrays. A program takes and returns all parts, laid end to end along the dimension named above; an argument that names none is the same for every part. Nothing has to cross between parts.
Inputs may be any that keep to these rules, and one draw needn't show every extreme that they name: strain stays within the stated range. Row b of neighbours names b first, then b - 1 and b + 1 (-1 where outside the fibre), then further blocks at most 2 away from b, or -1; entries may repeat; the number of named blocks differs from row to row; some row names a block exactly 2 away.
All inputs are finite; a program needn't handle non-finite values.
Results may differ from the reference program's by a relative error of at most 0.012.
The reference program's roundings to bfloat16 on the way count: a program that leaves them out, or rounds other values in their place, can miss the bound.
Values may be sent and summed in bfloat16 or wider, within the bound.
A program may use at most 64 MiB of HBM per device.

```python
import jax
import jax.numpy as jnp
from jax import lax

MODEL_WIDTH = 1024
ATTENTION_HEADS = 16
HEAD_SIZE = 64
E = 256
PATCHES_IN_BLOCK = 128
PC = 8
PT = 16
NBMAX = 6
NSEIS = 32
CHANNEL_BLOCKS = 4
REACH = 2
NCP = 512
TIME_PATCHES = 4
NT = 64
NCH = 4096


def draw_strain(key, part):
    amplitude = 3.0
    base = jnp.clip(jax.random.normal(key, (NT, NCH), jnp.float32), -2.6, 2.6)
    return (amplitude * base).astype(jnp.bfloat16)


def draw_attn_in(key, part):
    first = jax.random.fold_in(jax.random.fold_in(key, 23), 0)
    base = jnp.clip(jax.random.normal(first, (MODEL_WIDTH, 3 * MODEL_WIDTH), jnp.float32), -4.5, 4.5) / jnp.sqrt(jnp.float32(MODEL_WIDTH))
    return base.astype(jnp.bfloat16)


def draw_neighbours(key, part):
    first, second, third = jax.random.split(jax.random.fold_in(key, 11), 3)
    channel_blocks = jnp.arange(CHANNEL_BLOCKS, dtype=jnp.int32)
    left = jnp.where(channel_blocks > 0, channel_blocks - 1, -1)
    right = jnp.where(channel_blocks < CHANNEL_BLOCKS - 1, channel_blocks + 1, -1)
    offsets = jax.random.randint(first, (CHANNEL_BLOCKS, NBMAX - 3), -REACH, REACH + 1, dtype=jnp.int32)
    keep = jax.random.randint(second, (CHANNEL_BLOCKS, NBMAX - 3), 0, 5, dtype=jnp.int32) < 3
    busiest = jax.random.randint(third, (), 0, CHANNEL_BLOCKS, dtype=jnp.int32)
    chosen_row = channel_blocks[:, None] == busiest
    keep = keep | chosen_row
    farthest = jnp.where(busiest + REACH <= CHANNEL_BLOCKS - 1, REACH, -REACH).astype(jnp.int32)
    first_slot = jnp.arange(NBMAX - 3, dtype=jnp.int32)[None, :] == 0
    offsets = jnp.where(chosen_row & first_slot, farthest, offsets)
    targets = channel_blocks[:, None] + offsets
    inside = (targets >= 0) & (targets < CHANNEL_BLOCKS)
    extras = jnp.where(keep & inside, targets, -1)
    return jnp.concatenate([channel_blocks[:, None], left[:, None], right[:, None], extras], axis=1).astype(jnp.int32)


def touch_ends(entries, own_key, low, top_value):
    longest = entries.shape.index(max(entries.shape))
    spots = []
    for shift in (0, 1):
        where = [jax.random.randint(jax.random.fold_in(own_key, axis), (), 0, length) for axis, length in enumerate(entries.shape)]
        where[longest] = (where[longest] + shift) % entries.shape[longest]
        spots.append(tuple(where))
    return entries.at[spots[0]].set(low).at[spots[1]].set(top_value)


def scatter_about(rng, shape, scale, bound, held_as=jnp.bfloat16):
    entries = jax.random.normal(rng, shape, jnp.float32) * scale
    return jnp.minimum(jnp.maximum(entries, -bound), bound).astype(held_as)


def setup_inputs(seed: int = 0, part: int = 0) -> dict:
    key_list = jax.random.split(jax.random.key(seed), 9)
    part_splits = jax.random.split(jax.random.fold_in(key_list[8], part), 9)
    strain = draw_strain(jax.random.fold_in(jax.random.fold_in(key_list[8], part), 71), part)
    stem_weight = scatter_about(key_list[1], ((PT + 2) * (PC + 2), MODEL_WIDTH), ((PT + 2) * (PC + 2)) ** -0.5, 0.4375)
    attn_in = draw_attn_in(jax.random.fold_in(key_list[8], 71), part)
    attn_out = scatter_about(key_list[3], (MODEL_WIDTH, MODEL_WIDTH), MODEL_WIDTH ** -0.5, 0.1875)
    pool_weight = scatter_about(key_list[4], (MODEL_WIDTH, E), MODEL_WIDTH ** -0.5, 0.1875)
    neighbours = draw_neighbours(jax.random.fold_in(jax.random.fold_in(key_list[8], part), 71), part)
    seismo_embed = scatter_about(part_splits[6], (NSEIS, E), 1.0, 6.0, jnp.float32)
    colocated = touch_ends(jax.random.randint(part_splits[7], (NSEIS,), 0, CHANNEL_BLOCKS), jax.random.fold_in(part_splits[7], 1), 0, CHANNEL_BLOCKS - 1).astype(jnp.int32)
    return {"strain": strain, "stem_weight": stem_weight, "attn_in": attn_in, "attn_out": attn_out, "pool_weight": pool_weight, "neighbours": neighbours, "seismo_embed": seismo_embed, "colocated": colocated}


def attend_head(query_head, key_head, value_head, allowed):
    scores = jnp.dot(query_head, key_head.T, preferred_element_type=jnp.float32) / jnp.sqrt(jnp.float32(HEAD_SIZE))
    scores = jnp.where(allowed[None, :], scores, -jnp.inf)
    peak = lax.optimization_barrier(jnp.max(scores, axis=1, keepdims=True))
    weights = jnp.where(allowed[None, :], jnp.exp(scores - peak), jnp.float32(0.0))
    total = lax.optimization_barrier(jnp.sum(weights, axis=1, keepdims=True))
    mixed_output = jnp.dot(weights.astype(jnp.bfloat16), value_head, preferred_element_type=jnp.float32)
    return (mixed_output / total).astype(jnp.bfloat16)

def reference(strain, stem_weight, attn_in, attn_out, pool_weight, neighbours, seismo_embed, colocated):
    padded = jnp.pad(strain, 1)
    kernel = stem_weight.T.reshape(MODEL_WIDTH, 1, PT + 2, PC + 2)
    stem = lax.conv_general_dilated(padded[None, None], kernel, (PT, PC), 'VALID', dimension_numbers=('NCHW', 'OIHW', 'NHWC'), preferred_element_type=jnp.float32)[0]
    tokens = stem.astype(jnp.bfloat16)
    mixed_output = jnp.dot(tokens.reshape(TIME_PATCHES * NCP, MODEL_WIDTH), attn_in, preferred_element_type=jnp.float32).astype(jnp.bfloat16)
    mixed_output = mixed_output.reshape(TIME_PATCHES, CHANNEL_BLOCKS, PATCHES_IN_BLOCK, 3, ATTENTION_HEADS, HEAD_SIZE)
    channel_blocks = mixed_output.transpose(1, 0, 2, 3, 4, 5).reshape(CHANNEL_BLOCKS, TIME_PATCHES * PATCHES_IN_BLOCK, 3, ATTENTION_HEADS, HEAD_SIZE)
    queries_per_group = TIME_PATCHES * PATCHES_IN_BLOCK
    slots = jnp.arange(NBMAX, dtype=jnp.int32)
    earlier = slots[None, :] < slots[:, None]

    def one_block(index):
        row = neighbours[index]
        repeat = jnp.any((row[:, None] == row[None, :]) & earlier, axis=1)
        valid = (row >= 0) & jnp.logical_not(repeat)
        chosen = jnp.take(channel_blocks, jnp.clip(row, 0, CHANNEL_BLOCKS - 1).astype(jnp.int32), axis=0)
        keys_all = chosen[:, :, 1].reshape(NBMAX * queries_per_group, ATTENTION_HEADS, HEAD_SIZE).transpose(1, 0, 2)
        values_all = chosen[:, :, 2].reshape(NBMAX * queries_per_group, ATTENTION_HEADS, HEAD_SIZE).transpose(1, 0, 2)
        allowed = jnp.repeat(valid, queries_per_group)
        queries = lax.dynamic_index_in_dim(channel_blocks, index, 0, keepdims=False)[:, 0].transpose(1, 0, 2)
        return lax.map(lambda trio: attend_head(trio[0], trio[1], trio[2], allowed), (queries, keys_all, values_all))
    attended_output = lax.map(one_block, jnp.arange(CHANNEL_BLOCKS, dtype=jnp.int32))
    attended_output = attended_output.transpose(0, 2, 1, 3).reshape(CHANNEL_BLOCKS, TIME_PATCHES, PATCHES_IN_BLOCK, MODEL_WIDTH).transpose(1, 0, 2, 3)
    branch = jnp.dot(attended_output.reshape(TIME_PATCHES * NCP, MODEL_WIDTH), attn_out, preferred_element_type=jnp.float32).reshape(TIME_PATCHES, NCP, MODEL_WIDTH)
    encoded = (tokens.astype(jnp.float32) + branch).astype(jnp.bfloat16)
    pooled_output = lax.optimization_barrier(jnp.mean(encoded.astype(jnp.float32).reshape(TIME_PATCHES, CHANNEL_BLOCKS, PATCHES_IN_BLOCK, MODEL_WIDTH), axis=(0, 2))).astype(jnp.bfloat16)
    projected = jnp.dot(pooled_output, pool_weight, preferred_element_type=jnp.float32)
    block_embed = projected / jnp.sqrt(lax.optimization_barrier(jnp.sum(projected * projected, axis=1, keepdims=True)) + 1e-06)
    seismo_unit = seismo_embed / jnp.sqrt(lax.optimization_barrier(jnp.sum(seismo_embed * seismo_embed, axis=1, keepdims=True)) + 1e-06)
    logits = 50.0 * jnp.dot(seismo_unit, block_embed.T, precision=lax.Precision.HIGHEST)
    spread = jnp.log(lax.optimization_barrier(jnp.sum(jnp.exp(logits), axis=1)))
    matches = colocated[:, None] == jnp.arange(CHANNEL_BLOCKS, dtype=jnp.int32)[None, :]
    label = lax.optimization_barrier(jnp.sum(jnp.where(matches, logits, jnp.float32(0.0)), axis=1))
    return (encoded, spread - label)
```

```python
import functools

import jax
import jax.numpy as jnp
import numpy as np
from jax import lax
from jax.experimental import pallas as pl
from jax.experimental.pallas import tpu as pltpu
from jax.sharding import PartitionSpec as P

HEAD_SIZE = 64
PC = 8
PT = 16
REACH = 3
MESH = pl.DeviceIdType.MESH
F32 = jnp.float32
BF16 = jnp.bfloat16
NT_DIMS = (((1,), (1,)), ((), ()))


def tap_tables():
    place = np.zeros((256, (PT + 2) * (PC + 2)), np.float32)
    pick = np.zeros((128, 128), np.float32)
    tap = lambda i, j: (i + 1) * (PC + 2) + j + 1
    lane = lambda i, j: j * PT + i
    for i in range(PT):
        for j in range(PC):
            place[lane(i, j), tap(i, j)] = 1
        place[128 + 112 + i, tap(i, -1)] = 1
        place[128 + i, tap(i, PC)] = 1
    for j in range(PC):
        place[128 + 16 + j, tap(-1, j)] = 1
        place[128 + 32 + j, tap(PT, j)] = 1
        pick[lane(PT - 1, j), 16 + j] = 1
        pick[lane(0, j), 32 + j] = 1
    corners = ((48, -1, -1), (49, -1, PC), (50, PT, -1), (51, PT, PC))
    for at, i, j in corners:
        place[128 + at, tap(i, j)] = 1
        pick[lane(i % PT, j % PC), at] = 1
    return place, pick


def layer(
    sizes,
    strain_hbm,
    stem_hbm,
    attn_in_ref,
    attn_out_ref,
    pool_ref,
    place_hbm,
    pick_hbm,
    neighbours_hbm,
    seismo_hbm,
    colocated_hbm,
    encoded_hbm,
    loss_hbm,
    tiles,
    picked,
    tokens_own,
    queries,
    keys,
    values,
    attended,
    received,
    sums,
    embeds,
    w_query,
    w_key,
    w_value,
    w_out,
    w_pool,
    strain_ref,
    stem_ref,
    place_ref,
    pick_ref,
    seismo_ref,
    colocated_ref,
    encoded_ref,
    loss_ref,
    neighbours_ref,
    w_sem,
    chan_sems,
    tm_sems,
    head_sems,
    swap_sems,
    sum_sems,
    embed_sems,
):
    chans, tms, heads, block, slab, width, gathered, reach_slots = sizes
    times = tms * heads
    own = gathered // 2
    rows = gathered * block
    chan = lax.axis_index("chan")
    tm = lax.axis_index("tm")
    head = lax.axis_index("head")
    group = tm * heads + head

    barrier = pltpu.get_barrier_semaphore()
    flat = chans * times <= 16
    peers = [(far, step) for far in range(chans) for step in range(times)]
    peers = [pair for pair in peers if (all(pair) and flat) or (any(pair) and not all(pair))]

    peers = sorted(peers, key=lambda pair: -min(pair[0], chans - pair[0]))

    def device(far, step):
        peer = lax.rem(group + step, times)
        return {
            "chan": lax.rem(chan + far, chans),
            "tm": peer // heads,
            "head": lax.rem(peer, heads),
        }

    for far, step in peers:
        pl.semaphore_signal(barrier, inc=1, device_id=device(far, step), device_id_type=MESH)

    first = pltpu.make_async_copy(strain_hbm, strain_ref, w_sem.at[5])
    first.start()
    small = []
    for number, (source, buffer) in enumerate(
        (
            (stem_hbm, stem_ref),
            (place_hbm, place_ref),
            (pick_hbm, pick_ref),
            (neighbours_hbm, neighbours_ref),
            (seismo_hbm, seismo_ref),
            (colocated_hbm, colocated_ref),
        )
    ):
        small.append(pltpu.make_async_copy(source, buffer, w_sem.at[6 + number]))
        small[-1].start()
    column = pl.multiple_of(group * slab, slab)
    loads = []
    for number, buffer in enumerate((w_query, w_key, w_value)):
        source = attn_in_ref.at[:, pl.ds(number * width + column, slab)]
        loads.append(pltpu.make_async_copy(source, buffer, w_sem.at[number]))
    loads.append(pltpu.make_async_copy(attn_out_ref, w_out, w_sem.at[3]))
    loads.append(pltpu.make_async_copy(pool_ref, w_pool, w_sem.at[4]))
    for load in loads:
        load.start()

    lanes16 = lax.broadcasted_iota(jnp.int32, (PT, 128), 1)
    rows16 = lax.broadcasted_iota(jnp.int32, (PT, 128), 0)
    spread_eye = jnp.where(lax.rem(lanes16, PT) == rows16, 1.0, 0.0).astype(BF16)
    first.wait()
    spread = lax.dot_general(
        strain_ref[...], spread_eye, (((0,), (0,)), ((), ())), preferred_element_type=F32
    )
    sample = lax.rem(lax.broadcasted_iota(jnp.int32, spread.shape, 0), PC)
    slot = lax.broadcasted_iota(jnp.int32, spread.shape, 1) // PT
    spread = jnp.where(sample == slot, spread, 0.0)
    tiles[group, own] = jnp.sum(spread.reshape(block, PC, 128), axis=1).astype(BF16)

    pl.semaphore_wait(barrier, len(peers))

    started = []

    def send(source, target, sems, number, device):
        copy = pltpu.make_async_remote_copy(
            src_ref=source,
            dst_ref=target,
            send_sem=sems.at[0, number],
            recv_sem=sems.at[1, number],
            device_id=device,
            device_id_type=MESH,
        )
        copy.start()
        started.append(copy)
        return copy

    def forward(place):
        copies = []
        for step in range(1, tms):
            copies.append(
                send(
                    tiles.at[group, place],
                    tiles.at[group, place],
                    tm_sems,
                    (step - 1) * gathered + place,
                    {"tm": lax.rem(tm + step, tms)},
                )
            )
        return copies

    if gathered == chans:
        steps = sorted(range(1, chans), key=lambda d: min(d, chans - d))
    else:
        steps = [d % chans for far in range(1, own + 1) for d in (far, -far)]
    from_chan = []
    for number, step in enumerate(steps):
        place = (own - step) % chans
        from_chan.append(
            (
                place,
                send(
                    tiles.at[group, own],
                    tiles.at[group, place],
                    chan_sems,
                    number,
                    {"chan": lax.rem(chan + step, chans)},
                ),
            )
        )
    from_tm = forward(own)
    for load in small:
        load.wait()
    stem = jnp.dot(place_ref[...], stem_ref[...], preferred_element_type=F32).astype(BF16)
    for place, copy in from_chan:
        copy.wait_recv()
        from_tm += forward(place)
    from_head = []

    def share(time_row, number):
        for step in range(1, heads):
            from_head.append(
                send(
                    tiles.at[time_row],
                    tiles.at[time_row],
                    head_sems,
                    number * (heads - 1) + step - 1,
                    {"head": lax.rem(head + step, heads)},
                )
            )

    share(group, 0)
    for step in range(1, tms):
        for copy in from_tm[step - 1 :: tms - 1]:
            copy.wait_recv()
        share(lax.rem(tm + tms - step, tms) * heads + head, step)
    for load in loads[:3]:
        load.wait()
    for copy in from_head:
        copy.wait_recv()

    def pick_time(time, carry):
        flat = tiles[time].reshape(rows, 128)
        picked[time] = jnp.dot(flat, pick_ref[...], preferred_element_type=F32)
        return carry

    lax.fori_loop(0, times, pick_time, 0, unroll=True)
    lane = lax.broadcasted_iota(jnp.int32, (rows, 128), 1)
    row = lax.broadcasted_iota(jnp.int32, (rows, 128), 0)
    first_row = lax.rem(own - chan + chans, chans) * block
    last_row = lax.rem(own - chan + chans + chans - 1, chans) * block + block - 1
    low, high = reach_slots[0], reach_slots[-1] + 1

    def project(time, carry):
        here = tiles[time].reshape(rows, 128)
        here32 = here.astype(F32)
        above = picked[jnp.maximum(time - 1, 0)] * jnp.where(time > 0, 1.0, 0.0)
        below = picked[jnp.minimum(time + 1, times - 1)] * jnp.where(time < times - 1, 1.0, 0.0)
        left = jnp.where(
            lane >= 112, here32, jnp.where(lane == 48, above, jnp.where(lane == 50, below, 0.0))
        )
        right = jnp.where(
            lane < 16, here32, jnp.where(lane == 49, above, jnp.where(lane == 51, below, 0.0))
        )
        left = jnp.where(row == first_row, 0.0, pltpu.roll(left, 1, 0))
        right = jnp.where(row == last_row, 0.0, pltpu.roll(right, rows - 1, 0))
        middle = jnp.where(
            (lane >= 16) & (lane < 24), above, jnp.where((lane >= 32) & (lane < 40), below, 0.0)
        )
        halo = (left + right + middle).astype(BF16)
        taps = jnp.concatenate([here, halo], axis=1)[low * block : high * block]
        tokens = jnp.dot(taps, stem, preferred_element_type=F32).astype(BF16)
        mine = tokens[(own - low) * block : (own - low + 1) * block]
        tokens_own[time] = mine
        query = jnp.dot(mine, w_query[...], preferred_element_type=F32).astype(BF16) * BF16(0.125)
        key = jnp.dot(tokens, w_key[...], preferred_element_type=F32).astype(BF16)
        value = jnp.dot(tokens, w_value[...], preferred_element_type=F32).astype(BF16)
        for pair in range(slab // 128):
            part = slice(pair * 128, pair * 128 + 128)
            queries[pair, time] = query[:, part]
            for number in range(high - low):
                span = slice(number * block, (number + 1) * block)
                keys[pair, number, time] = key[span, part]
                values[pair, number, time] = value[span, part]
        return carry

    lax.fori_loop(0, times, project, 0, unroll=2)

    biases = []
    for place in reach_slots:
        number = lax.rem(chan + place - own + chans, chans)
        listed = neighbours_ref[chan, 0] == number
        for entry in range(1, neighbours_ref.shape[1]):
            listed = listed | (neighbours_ref[chan, entry] == number)
        biases.append(jnp.where(listed, 0.0, -jnp.inf).astype(F32))

    batch = heads
    pairs = slab // 128
    span = batch * block
    half = lax.broadcasted_iota(jnp.int32, (span, 128), 1) < HEAD_SIZE

    def attend(chunk, pair, carry):
        both = queries[pair, pl.ds(chunk * batch, batch)].reshape(span, 128)
        results = []
        for keep in (half, jnp.logical_not(half)):
            query = jnp.where(keep, both, jnp.zeros_like(both))
            scores, tops = [], []
            for number, bias in enumerate(biases):
                key = keys[pair, number].reshape(times * block, 128)
                score = lax.dot_general(query, key, NT_DIMS, preferred_element_type=F32)
                scores.append(score)
                tops.append(jnp.max(score, axis=1, keepdims=True) + bias)
            peak = functools.reduce(jnp.maximum, tops)
            total = jnp.zeros((span, 1), F32)
            output = jnp.zeros((span, 128), F32)
            for number, bias in enumerate(biases):
                weights = jnp.exp(scores[number] - (peak - bias))
                total = total + jnp.sum(weights, axis=1, keepdims=True)
                value = values[pair, number].reshape(times * block, 128)
                output = output + jnp.dot(
                    weights.astype(BF16), value, preferred_element_type=F32
                )
            results.append(output / total)
        merged = jnp.where(half, results[0], results[1]).astype(BF16)
        attended[pl.ds(chunk * batch, batch), pair] = merged.reshape(batch, block, 128)
        return carry

    swaps = []
    for far in range(1, tms + 1):
        chunk = lax.rem(tm + far, tms)
        lax.fori_loop(0, pairs, functools.partial(attend, chunk), 0)
        for step in range(0 if far < tms else 1, heads):
            to_head = lax.rem(head + step, heads)
            swaps.append(
                send(
                    attended.at[chunk * heads + to_head],
                    received.at[group],
                    swap_sems,
                    far % tms * heads + step,
                    {"tm": chunk, "head": to_head},
                )
            )
    def exchange(buffer, near, sems):
        copies = []
        for number, (far, step) in enumerate(near):
            copies.append(send(buffer, buffer, sems, number, device(far, step)))
        return copies

    for pair in range(pairs):
        part = attended[:, pair].reshape(times * block, 128).astype(F32)
        sums[chan, group, pair] = jnp.sum(part, axis=0, keepdims=True)
        lanes = pl.ds(pl.multiple_of(column + pair * 128, 128), 128)
        part = tokens_own[:, :, lanes].reshape(times * block, 128).astype(F32)
        sums[chan, group, pairs + pair] = jnp.sum(part, axis=0, keepdims=True)
    if flat:
        near = sorted(peers, key=lambda pair: -pair[0] * (chans - pair[0]))
    else:
        near = [pair for pair in peers if pair[0] == 0]
    totals = exchange(sums.at[chan, group], near, sum_sems)
    received[group] = attended[group]
    for load in loads[3:]:
        load.wait()
    for copy in swaps:
        copy.wait_recv()
    merged = jnp.concatenate(
        [received[time, pair] for time in range(times) for pair in range(pairs)], axis=1
    )
    branch = jnp.dot(merged, w_out[...], preferred_element_type=F32)
    encoded_ref[...] = (tokens_own[group].astype(F32) + branch).astype(BF16)
    write = pltpu.make_async_copy(encoded_ref, encoded_hbm, w_sem.at[12])
    write.start()

    seismo = seismo_ref[...]
    unit = seismo / jnp.sqrt(jnp.sum(seismo * seismo, axis=1, keepdims=True) + 1e-06)
    for copy in totals:
        copy.wait_recv()

    numbers = range(chans) if flat else [chan]

    def assemble(first):
        rows = []
        for number in numbers:
            parts = [sums[number, g, first + pair] for g in range(times) for pair in range(pairs)]
            rows.append(jnp.concatenate(parts, axis=1))
        return jnp.concatenate(rows, axis=0) / (times * block)

    mean = assemble(0)
    coarse = mean.astype(BF16)
    fine = (mean - coarse.astype(F32)).astype(BF16)
    mixed = jnp.dot(
        jnp.concatenate([coarse, fine], axis=0), w_out[...], preferred_element_type=F32
    )
    pooled = assemble(pairs) + mixed[: len(numbers)] + mixed[len(numbers) :]
    projected = jnp.dot(pooled.astype(BF16), w_pool[...], preferred_element_type=F32)
    every = projected / jnp.sqrt(
        jnp.sum(projected * projected, axis=1, keepdims=True) + 1e-06
    )
    if not flat:
        embeds[chan] = every
        near = [pair for pair in peers if pair[1] == 0]
        for copy in exchange(embeds.at[chan], near, embed_sems):
            copy.wait_recv()
        every = jnp.concatenate([embeds[number] for number in range(chans)], axis=0)
    logits = 50.0 * lax.dot_general(
        every, unit, NT_DIMS, precision=lax.Precision.HIGHEST, preferred_element_type=F32
    )
    spread = jnp.log(jnp.sum(jnp.exp(logits), axis=0, keepdims=True))
    matches = lax.broadcasted_iota(jnp.int32, logits.shape, 0) == colocated_ref[...]
    label = jnp.sum(jnp.where(matches, logits, 0.0), axis=0, keepdims=True)
    loss_ref[...] = spread - label
    store = pltpu.make_async_copy(loss_ref, loss_hbm, w_sem.at[13])
    store.start()
    write.wait()
    store.wait()
    for copy in started:
        copy.wait_send()


def hand_over(encoded_ref, loss_ref, encoded_out, loss_out):
    encoded_out[...] = encoded_ref[...]
    loss_out[...] = loss_ref[...]


def on_device(
    strain, stem_weight, attn_in, attn_out, pool_weight, neighbours, seismo_embed, colocated
):
    chans, tms, heads = (lax.axis_size(axis) for axis in ("chan", "tm", "head"))
    times = tms * heads
    width = attn_in.shape[0]
    slab = width // times
    pairs = slab // 128
    block = strain.shape[1] // PC
    wide = 2 * (REACH + 1) + 1
    gathered = chans if chans <= wide else wide
    reach_slots = range(gathered) if gathered == chans else range(1, gathered - 1)
    reached = len(reach_slots)
    place, pick = tap_tables()
    vmem = pl.BlockSpec(memory_space=pltpu.VMEM)
    hbm = pl.BlockSpec(memory_space=pl.ANY)
    dma = pltpu.SemaphoreType.DMA
    sizes = (chans, tms, heads, block, slab, width, gathered, reach_slots)
    shapes = (
        jax.ShapeDtypeStruct((block, width), BF16),
        jax.ShapeDtypeStruct((1, seismo_embed.shape[0]), F32),
    )
    encoded, loss = pl.pallas_call(
        functools.partial(layer, sizes),
        out_shape=shapes,
        in_specs=[hbm] * 10,
        out_specs=(hbm, hbm),
        scratch_shapes=[
            pltpu.VMEM((times, gathered, block, 128), BF16),
            pltpu.VMEM((times, gathered * block, 128), F32),
            pltpu.VMEM((times, block, width), BF16),
            pltpu.VMEM((pairs, times, block, 128), BF16),
            pltpu.VMEM((pairs, reached, times, block, 128), BF16),
            pltpu.VMEM((pairs, reached, times, block, 128), BF16),
            pltpu.VMEM((times, pairs, block, 128), BF16),
            pltpu.VMEM((times, pairs, block, 128), BF16),
            pltpu.VMEM((chans, times, 2 * pairs, 1, 128), F32),
            pltpu.VMEM((chans, 1, pool_weight.shape[1]), F32),
            pltpu.VMEM((width, slab), BF16),
            pltpu.VMEM((width, slab), BF16),
            pltpu.VMEM((width, slab), BF16),
            pltpu.VMEM(attn_out.shape, BF16),
            pltpu.VMEM(pool_weight.shape, BF16),
            pltpu.VMEM(strain.shape, BF16),
            pltpu.VMEM(stem_weight.shape, BF16),
            pltpu.VMEM(place.shape, BF16),
            pltpu.VMEM(pick.shape, BF16),
            pltpu.VMEM(seismo_embed.shape, F32),
            pltpu.VMEM((1, seismo_embed.shape[0]), jnp.int32),
            pltpu.VMEM((block, width), BF16),
            pltpu.VMEM((1, seismo_embed.shape[0]), F32),
            pltpu.SMEM(neighbours.shape, jnp.int32),
            dma((14,)),
            dma((2, gathered - 1)),
            dma((2, (tms - 1) * gathered)),
            dma((2, tms * (heads - 1))),
            dma((2, times)),
            dma((2, chans * times)),
            dma((2, chans)),
        ],
        compiler_params=pltpu.CompilerParams(
            collective_id=0, has_side_effects=True, vmem_limit_bytes=56 * 1024 * 1024
        ),
    )(
        strain,
        stem_weight,
        attn_in,
        attn_out,
        pool_weight,
        jnp.asarray(place, BF16),
        jnp.asarray(pick, BF16),
        neighbours,
        seismo_embed,
        colocated[None, :],
    )
    encoded, loss = pl.pallas_call(
        hand_over,
        out_shape=shapes,
        in_specs=[vmem, vmem],
        out_specs=(vmem, vmem),
    )(encoded, loss)
    return (encoded[None], loss[0])


def solution(mesh):
    in_specs = (
        P(("grp", "tm", "head"), "chan"),
        P(),
        P(),
        P(),
        P(),
        P("grp", None),
        P("grp", None),
        P("grp"),
    )
    out_specs = (P(("grp", "tm", "head"), "chan", None), P("grp"))
    return jax.shard_map(
        on_device, mesh=mesh, in_specs=in_specs, out_specs=out_specs, check_vma=False
    )
```

```python
import functools

import jax
import jax.numpy as jnp
import numpy as np
from jax import lax
from jax.experimental import pallas as pl
from jax.experimental.pallas import tpu as pltpu
from jax.sharding import PartitionSpec as P

HEAD_SIZE = 64
PC = 8
PT = 16
EDGE = 16
MESH = pl.DeviceIdType.MESH
F32 = jnp.float32
BF16 = jnp.bfloat16
NT_DIMS = (((1,), (1,)), ((), ()))


def tap_tables():
    place = np.zeros((256, (PT + 2) * (PC + 2)), np.float32)
    pick = np.zeros((128, 128), np.float32)
    tap = lambda i, j: (i + 1) * (PC + 2) + j + 1
    lane = lambda i, j: j * PT + i
    for i in range(PT):
        for j in range(PC):
            place[lane(i, j), tap(i, j)] = 1
        place[128 + 112 + i, tap(i, -1)] = 1
        place[128 + i, tap(i, PC)] = 1
    for j in range(PC):
        place[128 + 16 + j, tap(-1, j)] = 1
        place[128 + 32 + j, tap(PT, j)] = 1
        pick[lane(PT - 1, j), 16 + j] = 1
        pick[lane(0, j), 32 + j] = 1
    corners = ((48, -1, -1), (49, -1, PC), (50, PT, -1), (51, PT, PC))
    for at, i, j in corners:
        place[128 + at, tap(i, j)] = 1
        pick[lane(i % PT, j % PC), at] = 1
    return place, pick


def layer(
    sizes,
    strain_hbm,
    stem_hbm,
    attn_in_ref,
    attn_out_ref,
    pool_ref,
    place_hbm,
    pick_hbm,
    neighbours_hbm,
    seismo_hbm,
    colocated_hbm,
    encoded_hbm,
    loss_hbm,
    tiles,
    tokens_own,
    queries,
    keys,
    values,
    attended,
    received,
    sums,
    embeds,
    w_query,
    w_key,
    w_value,
    w_out,
    w_pool,
    strain_ref,
    raw_ref,
    stem_ref,
    place_ref,
    pick_ref,
    seismo_ref,
    colocated_ref,
    encoded_ref,
    loss_ref,
    neighbours_ref,
    w_sem,
    tile_sems,
    head_sems,
    swap_sems,
    sum_sems,
    embed_sems,
):
    chans, tms, heads, block, slab, width, own, most = sizes
    times = tms * heads
    pairs = slab // 128
    reach = own - 1
    chan = lax.axis_index("chan")
    tm = lax.axis_index("tm")
    head = lax.axis_index("head")
    group = tm * heads + head

    barrier = pltpu.get_barrier_semaphore()
    flat = chans * times <= 16
    peers = [(far, step) for far in range(chans) for step in range(times)]
    peers = [
        pair
        for pair in peers
        if any(pair)
        and (flat or not all(pair) or (pair[1] % heads == 0 and min(pair[0], chans - pair[0]) <= own))
    ]

    peers = sorted(peers, key=lambda pair: -min(pair[0], chans - pair[0]))

    def device(far, step):
        peer = lax.rem(group + step, times)
        return {
            "chan": lax.rem(chan + far, chans),
            "tm": peer // heads,
            "head": lax.rem(peer, heads),
        }

    for far, step in peers:
        pl.semaphore_signal(barrier, inc=1, device_id=device(far, step), device_id_type=MESH)

    first = pltpu.make_async_copy(strain_hbm, strain_ref, w_sem.at[5])
    first.start()
    small = []
    for number, (source, buffer) in enumerate(
        (
            (stem_hbm, raw_ref),
            (place_hbm, place_ref),
            (pick_hbm, pick_ref),
            (neighbours_hbm, neighbours_ref),
            (seismo_hbm, seismo_ref),
            (colocated_hbm, colocated_ref),
        )
    ):
        small.append(pltpu.make_async_copy(source, buffer, w_sem.at[6 + number]))
        small[-1].start()
    column = pl.multiple_of(group * slab, slab)
    loads = []
    for number, buffer in enumerate((w_query, w_key, w_value)):
        source = attn_in_ref.at[:, pl.ds(number * width + column, slab)]
        loads.append(pltpu.make_async_copy(source, buffer, w_sem.at[number]))
    loads.append(pltpu.make_async_copy(attn_out_ref, w_out, w_sem.at[3]))
    loads.append(pltpu.make_async_copy(pool_ref, w_pool, w_sem.at[4]))
    for load in loads:
        load.start()

    lanes16 = lax.broadcasted_iota(jnp.int32, (PT, 128), 1)
    rows16 = lax.broadcasted_iota(jnp.int32, (PT, 128), 0)
    spread_eye = jnp.where(lax.rem(lanes16, PT) == rows16, 1.0, 0.0).astype(BF16)
    first.wait()
    spread = lax.dot_general(
        strain_ref[...], spread_eye, (((0,), (0,)), ((), ())), preferred_element_type=F32
    )
    sample = lax.rem(lax.broadcasted_iota(jnp.int32, spread.shape, 0), PC)
    slot = lax.broadcasted_iota(jnp.int32, spread.shape, 1) // PT
    spread = jnp.where(sample == slot, spread, 0.0)
    tiles[group, own] = jnp.sum(spread.reshape(block, PC, 128), axis=1).astype(BF16)

    pl.semaphore_wait(barrier, len(peers))

    started = []

    def send(source, target, sems, number, device):
        copy = pltpu.make_async_remote_copy(
            src_ref=source,
            dst_ref=target,
            send_sem=sems.at[0, number],
            recv_sem=sems.at[1, number],
            device_id=device,
            device_id_type=MESH,
        )
        copy.start()
        started.append(copy)
        return copy

    def shift(far, step, start):
        number = (far + own) * tms + step

        def tile(time_row):
            place = own - far
            if far == own:
                return tiles.at[time_row, place, pl.ds(block - EDGE, EDGE)]
            if far == -own:
                return tiles.at[time_row, place, pl.ds(0, EDGE)]
            return tiles.at[time_row, place]

        def outward():
            source = tiles.at[group, own]
            if abs(far) == own:
                source = tiles.at[group, own, pl.ds(block - EDGE if far > 0 else 0, EDGE)]
            return pltpu.make_async_remote_copy(
                src_ref=source,
                dst_ref=tile(group),
                send_sem=tile_sems.at[0, number],
                recv_sem=tile_sems.at[1, number],
                device_id={"chan": chan + far, "tm": lax.rem(tm + step, tms)},
                device_id_type=MESH,
            )

        def inward(from_step):
            row = lax.rem(tm + tms - step, tms) * heads + head
            return pltpu.make_async_remote_copy(
                src_ref=tile(row),
                dst_ref=tile(row),
                send_sem=head_sems.at[0, number * heads + from_step],
                recv_sem=head_sems.at[1, number * heads + from_step],
                device_id={"head": lax.rem(head + from_step, heads)},
                device_id_type=MESH,
            )

        here = (chan + far >= 0) & (chan + far < chans)
        there = (chan - far >= 0) & (chan - far < chans)
        local = far == 0 and step == 0

        def run(when, action):
            if far == 0:
                action()
            else:
                pl.when(when)(action)

        if start == "send" and not local:
            run(here, lambda: outward().start())
        if start == "pass":

            def relay():
                if not local:
                    outward().wait_recv()
                for from_step in range(1, heads):
                    inward(from_step).start()

            run(there, relay)
        if start == "take":

            def take():
                for from_step in range(1, heads):
                    inward(from_step).wait_recv()

            run(there, take)
        if start == "end":
            if not local:
                run(here, lambda: outward().wait_send())

            def done():
                for from_step in range(1, heads):
                    inward(from_step).wait_send()

            run(there, done)

    moves = [(far, step) for far in range(-own, own + 1) for step in range(tms)]
    moves = sorted(moves, key=lambda move: abs(move[0]) + move[1])
    close = [move for move in moves if abs(move[0]) <= 1]
    distant = [move for move in moves if abs(move[0]) > 1]
    for move in close + distant:
        shift(*move, "send")
    for load in small:
        load.wait()
    stem_ref[...] = jnp.dot(
        place_ref[...], raw_ref[...], preferred_element_type=F32
    ).astype(BF16)

    long = block + 2 * EDGE
    lane = lax.broadcasted_iota(jnp.int32, (long, 128), 1)
    toward = jnp.where(2 * chan < chans, -1, 1)
    numbers = [jnp.int32(0) * chan for _ in range(most)]
    count = jnp.int32(0) * chan
    for away in range(reach + 1):
        for side in (toward, -toward) if away else (toward,):
            number = chan + away * side
            valid = (number >= 0) & (number < chans)
            for index in range(most):
                numbers[index] = jnp.where(valid & (count == index), number, numbers[index])
            count = count + jnp.where(valid, 1, 0)

    def prepare(number):
        place = number - chan + own
        before = jnp.maximum(number - 1, 0) - chan + own
        after = jnp.minimum(number + 1, chans - 1) - chan + own
        has_before = jnp.where(number > 0, 1.0, 0.0)
        has_after = jnp.where(number < chans - 1, 1.0, 0.0)
        pieces, picks = [], []
        for time in range(times):
            head_rows = tiles[time, before, block - EDGE :]
            tail_rows = tiles[time, after, :EDGE]
            piece = jnp.concatenate([head_rows, tiles[time, place], tail_rows], axis=0)
            pieces.append(piece)
        picked = jnp.dot(
            jnp.concatenate(pieces, axis=0), pick_ref[...], preferred_element_type=F32
        )
        zeros = jnp.zeros((long, 128), F32)
        row = lax.broadcasted_iota(jnp.int32, (long, 128), 0)
        keep = jnp.where(row < EDGE, has_before, jnp.where(row >= EDGE + block, has_after, 1.0))
        taps = []
        for time in range(times):
            here32 = pieces[time].astype(F32)
            above = picked[(time - 1) * long : time * long] if time else zeros
            below = picked[(time + 1) * long : (time + 2) * long] if time < times - 1 else zeros
            left = jnp.where(
                lane >= 112, here32, jnp.where(lane == 48, above, jnp.where(lane == 50, below, 0.0))
            )
            right = jnp.where(
                lane < 16, here32, jnp.where(lane == 49, above, jnp.where(lane == 51, below, 0.0))
            )
            left = pltpu.roll(left * keep, 1, 0)[EDGE : EDGE + block]
            right = pltpu.roll(right * keep, long - 1, 0)[EDGE : EDGE + block]
            inner = lane[:block]
            middle = jnp.where(
                (inner >= 16) & (inner < 24),
                above[EDGE : EDGE + block],
                jnp.where((inner >= 32) & (inner < 40), below[EDGE : EDGE + block], 0.0),
            )
            halo = (left + right + middle).astype(BF16)
            taps.append(jnp.concatenate([pieces[time][EDGE : EDGE + block], halo], axis=1))
        return jnp.concatenate(taps, axis=0)

    def project(index, taps):
        return jnp.dot(taps, stem_ref[...], preferred_element_type=F32).astype(BF16)

    def keep_rows(index, tokens):
        key = jnp.dot(tokens, w_key[...], preferred_element_type=F32).astype(BF16)
        value = jnp.dot(tokens, w_value[...], preferred_element_type=F32).astype(BF16)
        for pair in range(pairs):
            part = slice(pair * 128, pair * 128 + 128)
            keys[pair, index] = key[:, part]
            values[pair, index] = value[:, part]

    def project_own():
        tokens = project(0, prepare(chan))
        tokens_own[...] = tokens.reshape(times, block, width)
        query = jnp.dot(tokens, w_query[...], preferred_element_type=F32).astype(BF16)
        query = query * BF16(0.125)
        for pair in range(pairs):
            queries[pair] = query[:, pair * 128 : pair * 128 + 128].reshape(times, block, 128)
        keep_rows(0, tokens)

    def project_rest(indices):
        taps = prepare(numbers[indices[0]])
        for at, index in enumerate(indices):
            tokens = project(index, taps)
            if at + 1 < len(indices):
                taps = prepare(numbers[indices[at + 1]])
            keep_rows(index, tokens)

    def project_or_clear(index):
        pl.when(count > index)(lambda: project_rest([index]))

        @pl.when(count <= index)
        def _():
            for pair in range(pairs):
                keys[pair, index] = jnp.zeros((times * block, 128), BF16)
                values[pair, index] = jnp.zeros((times * block, 128), BF16)

    for move in close:
        shift(*move, "pass")
    for load in loads[:3]:
        load.wait()
    for move in close:
        shift(*move, "take")
    project_own()
    for move in distant:
        shift(*move, "pass")
    if flat:

        @pl.when(count == most)
        def _():
            project_rest([1])

        for move in distant:
            shift(*move, "take")

        @pl.when(count == most)
        def _():
            project_rest(range(2, most))

        @pl.when(count < most)
        def _():
            project_rest(range(1, most - 1))
    else:
        for move in distant:
            shift(*move, "take")
        for index in range(1, most):
            project_or_clear(index)

    biases = []
    for index, number in enumerate(numbers):
        listed = neighbours_ref[chan, 0] == number
        for entry in range(1, neighbours_ref.shape[1]):
            listed = listed | (neighbours_ref[chan, entry] == number)
        listed = listed & (count > index)
        biases.append(jnp.where(listed, 0.0, -jnp.inf).astype(F32))

    batch = heads
    span = batch * block
    half = lax.broadcasted_iota(jnp.int32, (span, 128), 1) < HEAD_SIZE

    ones = jnp.ones((times * block, 128), BF16)
    span = block
    half = lax.broadcasted_iota(jnp.int32, (span, 128), 1) < HEAD_SIZE

    def attend(chunk, held):
        units = [(time, pair) for time in range(heads) for pair in range(pairs)]

        def stack(unit):
            time, pair = unit
            both = queries[pair, chunk * heads + time]
            blank = jnp.zeros_like(both)
            return jnp.concatenate(
                [jnp.where(half, both, blank), jnp.where(half, blank, both)], axis=0
            )

        def score(query, pair, number):
            return lax.dot_general(
                query, keys[pair, number], NT_DIMS, preferred_element_type=F32
            )

        query = stack(units[0])
        ahead = [score(query, units[0][1], number) for number in range(held)]
        for at, (time, pair) in enumerate(units):
            scores, ahead = ahead, []
            tops = [
                jnp.max(scores[number], axis=1, keepdims=True) + biases[number]
                for number in range(held)
            ]
            peak = functools.reduce(jnp.maximum, tops)
            if at + 1 < len(units):
                query = stack(units[at + 1])
            output = None
            for number in range(held):
                if at + 1 < len(units):
                    ahead.append(score(query, units[at + 1][1], number))
                weights = jnp.exp(scores[number] - (peak - biases[number])).astype(BF16)
                value = jnp.concatenate([values[pair, number], ones], axis=1)
                part = jnp.dot(weights, value, preferred_element_type=F32)
                output = part if output is None else output + part
            result = output[:, :128] / output[:, 128:]
            attended[chunk * heads + time, pair] = jnp.where(
                half, result[:span], result[span:]
            ).astype(BF16)

    counts = (most - 1, most) if flat else (most,)
    swaps = []
    for far in range(1, tms + 1):
        chunk = lax.rem(tm + far, tms)
        for held in counts:

            def each(held=held):
                attend(chunk, held)

            if len(counts) == 1:
                each()
            else:
                pl.when(count == held)(each)
        for step in range(0 if far < tms else 1, heads):
            to_head = lax.rem(head + step, heads)
            swaps.append(
                send(
                    attended.at[chunk * heads + to_head],
                    received.at[group],
                    swap_sems,
                    far % tms * heads + step,
                    {"tm": chunk, "head": to_head},
                )
            )
    def exchange(buffer, near, sems):
        copies = []
        for number, (far, step) in enumerate(near):
            copies.append(send(buffer, buffer, sems, number, device(far, step)))
        return copies

    for pair in range(pairs):
        part = attended[:, pair].reshape(times * block, 128).astype(F32)
        sums[chan, group, pair] = jnp.sum(part, axis=0, keepdims=True)
        lanes = pl.ds(pl.multiple_of(column + pair * 128, 128), 128)
        part = tokens_own[:, :, lanes].reshape(times * block, 128).astype(F32)
        sums[chan, group, pairs + pair] = jnp.sum(part, axis=0, keepdims=True)
    if flat:
        near = sorted(peers, key=lambda pair: -pair[0] * (chans - pair[0]))
    else:
        near = [pair for pair in peers if pair[0] == 0]
    totals = exchange(sums.at[chan, group], near, sum_sems)
    received[group] = attended[group]
    for load in loads[3:]:
        load.wait()
    for copy in swaps:
        copy.wait_recv()
    merged = jnp.concatenate(
        [received[time, pair] for time in range(times) for pair in range(pairs)], axis=1
    )
    branch = jnp.dot(merged, w_out[...], preferred_element_type=F32)
    encoded_ref[...] = (tokens_own[group].astype(F32) + branch).astype(BF16)
    write = pltpu.make_async_copy(encoded_ref, encoded_hbm, w_sem.at[12])
    write.start()

    seismo = seismo_ref[...]
    unit = seismo / jnp.sqrt(jnp.sum(seismo * seismo, axis=1, keepdims=True) + 1e-06)
    for copy in totals:
        copy.wait_recv()

    summed = range(chans) if flat else [chan]

    def assemble(first):
        rows = []
        for number in summed:
            parts = [sums[number, g, first + pair] for g in range(times) for pair in range(pairs)]
            rows.append(jnp.concatenate(parts, axis=1))
        return jnp.concatenate(rows, axis=0) / (times * block)

    mean = assemble(0)
    coarse = mean.astype(BF16)
    fine = (mean - coarse.astype(F32)).astype(BF16)
    mixed = jnp.dot(
        jnp.concatenate([coarse, fine], axis=0), w_out[...], preferred_element_type=F32
    )
    pooled = assemble(pairs) + mixed[: len(summed)] + mixed[len(summed) :]
    projected = jnp.dot(pooled.astype(BF16), w_pool[...], preferred_element_type=F32)
    every = projected / jnp.sqrt(
        jnp.sum(projected * projected, axis=1, keepdims=True) + 1e-06
    )
    if not flat:
        embeds[chan] = every
        near = [pair for pair in peers if pair[1] == 0]
        for copy in exchange(embeds.at[chan], near, embed_sems):
            copy.wait_recv()
        every = jnp.concatenate([embeds[number] for number in range(chans)], axis=0)
    logits = 50.0 * lax.dot_general(
        every, unit, NT_DIMS, precision=lax.Precision.HIGHEST, preferred_element_type=F32
    )
    spread = jnp.log(jnp.sum(jnp.exp(logits), axis=0, keepdims=True))
    matches = lax.broadcasted_iota(jnp.int32, logits.shape, 0) == colocated_ref[...]
    label = jnp.sum(jnp.where(matches, logits, 0.0), axis=0, keepdims=True)
    loss_ref[...] = spread - label
    store = pltpu.make_async_copy(loss_ref, loss_hbm, w_sem.at[13])
    store.start()
    write.wait()
    store.wait()
    for move in moves:
        shift(*move, "end")
    for copy in started:
        copy.wait_send()


def hand_over(encoded_ref, loss_ref, encoded_out, loss_out):
    encoded_out[...] = encoded_ref[...]
    loss_out[...] = loss_ref[...]


def on_device(
    strain, stem_weight, attn_in, attn_out, pool_weight, neighbours, seismo_embed, colocated
):
    chans, tms, heads = (lax.axis_size(axis) for axis in ("chan", "tm", "head"))
    times = tms * heads
    width = attn_in.shape[0]
    slab = width // times
    pairs = slab // 128
    block = strain.shape[1] // PC
    reach = 2 if chans <= 4 else 3
    own = reach + 1
    gathered = 2 * own + 1
    most = min(2 * reach + 1, chans)
    place, pick = tap_tables()
    vmem = pl.BlockSpec(memory_space=pltpu.VMEM)
    hbm = pl.BlockSpec(memory_space=pl.ANY)
    dma = pltpu.SemaphoreType.DMA
    sizes = (chans, tms, heads, block, slab, width, own, most)
    shapes = (
        jax.ShapeDtypeStruct((block, width), BF16),
        jax.ShapeDtypeStruct((1, seismo_embed.shape[0]), F32),
    )
    encoded, loss = pl.pallas_call(
        functools.partial(layer, sizes),
        out_shape=shapes,
        in_specs=[hbm] * 10,
        out_specs=(hbm, hbm),
        scratch_shapes=[
            pltpu.VMEM((times, gathered, block, 128), BF16),
            pltpu.VMEM((times, block, width), BF16),
            pltpu.VMEM((pairs, times, block, 128), BF16),
            pltpu.VMEM((pairs, most, times * block, 128), BF16),
            pltpu.VMEM((pairs, most, times * block, 128), BF16),
            pltpu.VMEM((times, pairs, block, 128), BF16),
            pltpu.VMEM((times, pairs, block, 128), BF16),
            pltpu.VMEM((chans, times, 2 * pairs, 1, 128), F32),
            pltpu.VMEM((chans, 1, pool_weight.shape[1]), F32),
            pltpu.VMEM((width, slab), BF16),
            pltpu.VMEM((width, slab), BF16),
            pltpu.VMEM((width, slab), BF16),
            pltpu.VMEM(attn_out.shape, BF16),
            pltpu.VMEM(pool_weight.shape, BF16),
            pltpu.VMEM(strain.shape, BF16),
            pltpu.VMEM(stem_weight.shape, BF16),
            pltpu.VMEM((256, width), BF16),
            pltpu.VMEM(place.shape, BF16),
            pltpu.VMEM(pick.shape, BF16),
            pltpu.VMEM(seismo_embed.shape, F32),
            pltpu.VMEM((1, seismo_embed.shape[0]), jnp.int32),
            pltpu.VMEM((block, width), BF16),
            pltpu.VMEM((1, seismo_embed.shape[0]), F32),
            pltpu.SMEM(neighbours.shape, jnp.int32),
            dma((14,)),
            dma((2, tms * gathered)),
            dma((2, tms * gathered * heads)),
            dma((2, times)),
            dma((2, chans * times)),
            dma((2, chans)),
        ],
        compiler_params=pltpu.CompilerParams(
            collective_id=0, has_side_effects=True, vmem_limit_bytes=56 * 1024 * 1024
        ),
    )(
        strain,
        stem_weight,
        attn_in,
        attn_out,
        pool_weight,
        jnp.asarray(place, BF16),
        jnp.asarray(pick, BF16),
        neighbours,
        seismo_embed,
        colocated[None, :],
    )
    encoded, loss = pl.pallas_call(
        hand_over,
        out_shape=shapes,
        in_specs=[vmem, vmem],
        out_specs=(vmem, vmem),
    )(encoded, loss)
    return (encoded[None], loss[0])


def solution(mesh):
    in_specs = (
        P(("grp", "tm", "head"), "chan"),
        P(),
        P(),
        P(),
        P(),
        P("grp", None),
        P("grp", None),
        P("grp"),
    )
    out_specs = (P(("grp", "tm", "head"), "chan", None), P("grp"))
    return jax.shard_map(
        on_device, mesh=mesh, in_specs=in_specs, out_specs=out_specs, check_vma=False
    )
```

```python
import functools

import jax
import jax.numpy as jnp
import numpy as np
from jax import lax
from jax.experimental import pallas as pl
from jax.experimental.pallas import tpu as pltpu
from jax.sharding import PartitionSpec as P

HEAD_SIZE = 64
PC = 8
PT = 16
EDGE = 16
MESH = pl.DeviceIdType.MESH
F32 = jnp.float32
BF16 = jnp.bfloat16
NT_DIMS = (((1,), (1,)), ((), ()))


def tap_tables():
    place = np.zeros((256, (PT + 2) * (PC + 2)), np.float32)
    pick = np.zeros((128, 128), np.float32)
    tap = lambda i, j: (i + 1) * (PC + 2) + j + 1
    lane = lambda i, j: j * PT + i
    for i in range(PT):
        for j in range(PC):
            place[lane(i, j), tap(i, j)] = 1
        place[128 + 112 + i, tap(i, -1)] = 1
        place[128 + i, tap(i, PC)] = 1
    for j in range(PC):
        place[128 + 16 + j, tap(-1, j)] = 1
        place[128 + 32 + j, tap(PT, j)] = 1
        pick[lane(PT - 1, j), 16 + j] = 1
        pick[lane(0, j), 32 + j] = 1
    corners = ((48, -1, -1), (49, -1, PC), (50, PT, -1), (51, PT, PC))
    for at, i, j in corners:
        place[128 + at, tap(i, j)] = 1
        pick[lane(i % PT, j % PC), at] = 1
    return place, pick


def layer(
    sizes,
    strain_hbm,
    stem_hbm,
    attn_in_ref,
    attn_out_ref,
    pool_ref,
    place_hbm,
    pick_hbm,
    neighbours_hbm,
    seismo_hbm,
    colocated_hbm,
    encoded_hbm,
    loss_hbm,
    tiles,
    tokens_own,
    queries,
    keys,
    values,
    attended,
    received,
    sums,
    embeds,
    w_query,
    w_key,
    w_value,
    w_out,
    w_pool,
    strain_ref,
    raw_ref,
    stem_ref,
    place_ref,
    pick_ref,
    seismo_ref,
    colocated_ref,
    encoded_ref,
    loss_ref,
    neighbours_ref,
    w_sem,
    far_sems,
    tile_sems,
    head_sems,
    swap_sems,
    sum_sems,
    embed_sems,
):
    chans, tms, heads, block, slab, width, own, most = sizes
    times = tms * heads
    pairs = slab // 128
    reach = own - 1
    chan = lax.axis_index("chan")
    tm = lax.axis_index("tm")
    head = lax.axis_index("head")
    group = tm * heads + head

    barrier = pltpu.get_barrier_semaphore()
    flat = chans * times <= 16
    peers = [(far, step) for far in range(chans) for step in range(times)]
    peers = [
        pair
        for pair in peers
        if any(pair)
        and (flat or not all(pair) or (pair[1] % heads == 0 and min(pair[0], chans - pair[0]) <= own))
    ]

    peers = sorted(peers, key=lambda pair: -min(pair[0], chans - pair[0]))

    def device(far, step):
        peer = lax.rem(group + step, times)
        return {
            "chan": lax.rem(chan + far, chans),
            "tm": peer // heads,
            "head": lax.rem(peer, heads),
        }

    def greet(far):
        for step in range(times):
            if far or step:
                peer = lax.rem(group + step, times)
                target = {"chan": chan + far, "tm": peer // heads, "head": lax.rem(peer, heads)}
                pl.semaphore_signal(barrier, inc=1, device_id=target, device_id_type=MESH)

    below, above = chan > 0, chan < chans - 1
    if flat:
        greet(0)
        pl.when(below)(lambda: greet(-1))
        pl.when(above)(lambda: greet(1))
    else:
        for far, step in peers:
            pl.semaphore_signal(barrier, inc=1, device_id=device(far, step), device_id_type=MESH)

    first = pltpu.make_async_copy(strain_hbm, strain_ref, w_sem.at[5])
    first.start()
    small = []
    for number, (source, buffer) in enumerate(
        (
            (stem_hbm, raw_ref),
            (place_hbm, place_ref),
            (pick_hbm, pick_ref),
            (neighbours_hbm, neighbours_ref),
            (seismo_hbm, seismo_ref),
            (colocated_hbm, colocated_ref),
        )
    ):
        small.append(pltpu.make_async_copy(source, buffer, w_sem.at[6 + number]))
        small[-1].start()
    column = pl.multiple_of(group * slab, slab)
    loads = []
    for number, buffer in enumerate((w_query, w_key, w_value)):
        source = attn_in_ref.at[:, pl.ds(number * width + column, slab)]
        loads.append(pltpu.make_async_copy(source, buffer, w_sem.at[number]))
    loads.append(pltpu.make_async_copy(attn_out_ref, w_out, w_sem.at[3]))
    loads.append(pltpu.make_async_copy(pool_ref, w_pool, w_sem.at[4]))
    for load in loads:
        load.start()

    lanes16 = lax.broadcasted_iota(jnp.int32, (PT, 128), 1)
    rows16 = lax.broadcasted_iota(jnp.int32, (PT, 128), 0)
    spread_eye = jnp.where(lax.rem(lanes16, PT) == rows16, 1.0, 0.0).astype(BF16)
    first.wait()
    spread = lax.dot_general(
        strain_ref[...], spread_eye, (((0,), (0,)), ((), ())), preferred_element_type=F32
    )
    sample = lax.rem(lax.broadcasted_iota(jnp.int32, spread.shape, 0), PC)
    slot = lax.broadcasted_iota(jnp.int32, spread.shape, 1) // PT
    spread = jnp.where(sample == slot, spread, 0.0)
    tiles[group, own] = jnp.sum(spread.reshape(block, PC, 128), axis=1).astype(BF16)

    for load in small:
        load.wait()
    stem_ref[...] = jnp.dot(
        place_ref[...], raw_ref[...], preferred_element_type=F32
    ).astype(BF16)

    def tell(sem, far):
        pl.semaphore_signal(sem, inc=1, device_id={"chan": chan + far}, device_id_type=MESH)

    def learn(hop):
        pl.when(chan >= hop)(lambda: pl.semaphore_wait(far_sems.at[0, hop - 2], 1))
        pl.when(chan + hop < chans)(lambda: pl.semaphore_wait(far_sems.at[1, hop - 2], 1))

    if flat:
        sides = jnp.where(below, times, 0) + jnp.where(above, times, 0)
        pl.semaphore_wait(barrier, times - 1 + sides)
    else:
        pl.semaphore_wait(barrier, len(peers))

    started = []

    def send(source, target, sems, number, device):
        copy = pltpu.make_async_remote_copy(
            src_ref=source,
            dst_ref=target,
            send_sem=sems.at[0, number],
            recv_sem=sems.at[1, number],
            device_id=device,
            device_id_type=MESH,
        )
        copy.start()
        started.append(copy)
        return copy

    def shift(far, step, start):
        number = (far + own) * tms + step

        def tile(time_row):
            place = own - far
            if far == own:
                return tiles.at[time_row, place, pl.ds(block - EDGE, EDGE)]
            if far == -own:
                return tiles.at[time_row, place, pl.ds(0, EDGE)]
            return tiles.at[time_row, place]

        def outward():
            source = tiles.at[group, own]
            if abs(far) == own:
                source = tiles.at[group, own, pl.ds(block - EDGE if far > 0 else 0, EDGE)]
            return pltpu.make_async_remote_copy(
                src_ref=source,
                dst_ref=tile(group),
                send_sem=tile_sems.at[0, number],
                recv_sem=tile_sems.at[1, number],
                device_id={"chan": chan + far, "tm": lax.rem(tm + step, tms)},
                device_id_type=MESH,
            )

        def inward(from_step):
            row = lax.rem(tm + tms - step, tms) * heads + head
            return pltpu.make_async_remote_copy(
                src_ref=tile(row),
                dst_ref=tile(row),
                send_sem=head_sems.at[0, number * heads + from_step],
                recv_sem=head_sems.at[1, number * heads + from_step],
                device_id={"head": lax.rem(head + from_step, heads)},
                device_id_type=MESH,
            )

        here = (chan + far >= 0) & (chan + far < chans)
        there = (chan - far >= 0) & (chan - far < chans)
        local = far == 0 and step == 0

        def run(when, action):
            if far == 0:
                action()
            else:
                pl.when(when)(action)

        if start == "send" and not local:
            run(here, lambda: outward().start())
        if start == "pass":

            def relay():
                if not local:
                    outward().wait_recv()
                for from_step in range(1, heads):
                    inward(from_step).start()

            run(there, relay)
        if start == "take":

            def take():
                for from_step in range(1, heads):
                    inward(from_step).wait_recv()

            run(there, take)
        if start == "end":
            if not local:
                run(here, lambda: outward().wait_send())

            def done():
                for from_step in range(1, heads):
                    inward(from_step).wait_send()

            run(there, done)

    moves = [(far, step) for far in range(-own, own + 1) for step in range(tms)]
    moves = sorted(moves, key=lambda move: abs(move[0]) + move[1])
    close = [move for move in moves if abs(move[0]) <= 1]
    distant = [move for move in moves if abs(move[0]) > 1]
    for move in close:
        shift(*move, "send")
    for hop in range(2, own + 1):
        if flat:
            if hop > 2:
                learn(hop - 1)
                for move in distant:
                    if abs(move[0]) == hop - 1:
                        shift(*move, "send")
            if hop < chans:
                pl.when((chan >= hop - 1) & above)(lambda: tell(far_sems.at[0, hop - 2], 1))
                pl.when((chan + hop <= chans) & below)(lambda: tell(far_sems.at[1, hop - 2], -1))
    if flat:
        learn(own)
    for move in distant:
        if abs(move[0]) == own or not flat:
            shift(*move, "send")
    long = block + 2 * EDGE
    lane = lax.broadcasted_iota(jnp.int32, (long, 128), 1)
    toward = jnp.where(2 * chan < chans, -1, 1)
    numbers = [jnp.int32(0) * chan for _ in range(most)]
    count = jnp.int32(0) * chan
    for away in range(reach + 1):
        for side in (toward, -toward) if away else (toward,):
            number = chan + away * side
            valid = (number >= 0) & (number < chans)
            for index in range(most):
                numbers[index] = jnp.where(valid & (count == index), number, numbers[index])
            count = count + jnp.where(valid, 1, 0)

    def prepare(number):
        place = number - chan + own
        before = jnp.maximum(number - 1, 0) - chan + own
        after = jnp.minimum(number + 1, chans - 1) - chan + own
        has_before = jnp.where(number > 0, 1.0, 0.0)
        has_after = jnp.where(number < chans - 1, 1.0, 0.0)
        pieces, picks = [], []
        for time in range(times):
            head_rows = tiles[time, before, block - EDGE :]
            tail_rows = tiles[time, after, :EDGE]
            piece = jnp.concatenate([head_rows, tiles[time, place], tail_rows], axis=0)
            pieces.append(piece)
        picked = jnp.dot(
            jnp.concatenate(pieces, axis=0), pick_ref[...], preferred_element_type=F32
        )
        zeros = jnp.zeros((long, 128), F32)
        row = lax.broadcasted_iota(jnp.int32, (long, 128), 0)
        keep = jnp.where(row < EDGE, has_before, jnp.where(row >= EDGE + block, has_after, 1.0))
        taps = []
        for time in range(times):
            here32 = pieces[time].astype(F32)
            above = picked[(time - 1) * long : time * long] if time else zeros
            below = picked[(time + 1) * long : (time + 2) * long] if time < times - 1 else zeros
            left = jnp.where(
                lane >= 112, here32, jnp.where(lane == 48, above, jnp.where(lane == 50, below, 0.0))
            )
            right = jnp.where(
                lane < 16, here32, jnp.where(lane == 49, above, jnp.where(lane == 51, below, 0.0))
            )
            left = pltpu.roll(left * keep, 1, 0)[EDGE : EDGE + block]
            right = pltpu.roll(right * keep, long - 1, 0)[EDGE : EDGE + block]
            inner = lane[:block]
            middle = jnp.where(
                (inner >= 16) & (inner < 24),
                above[EDGE : EDGE + block],
                jnp.where((inner >= 32) & (inner < 40), below[EDGE : EDGE + block], 0.0),
            )
            halo = (left + right + middle).astype(BF16)
            taps.append(jnp.concatenate([pieces[time][EDGE : EDGE + block], halo], axis=1))
        return jnp.concatenate(taps, axis=0)

    def project(index, taps):
        return jnp.dot(taps, stem_ref[...], preferred_element_type=F32).astype(BF16)

    def keep_rows(index, tokens):
        key = jnp.dot(tokens, w_key[...], preferred_element_type=F32).astype(BF16)
        value = jnp.dot(tokens, w_value[...], preferred_element_type=F32).astype(BF16)
        for pair in range(pairs):
            part = slice(pair * 128, pair * 128 + 128)
            keys[pair, index] = key[:, part]
            values[pair, index] = value[:, part]

    def project_own():
        tokens = project(0, prepare(chan))
        tokens_own[...] = tokens.reshape(times, block, width)
        query = jnp.dot(tokens, w_query[...], preferred_element_type=F32).astype(BF16)
        query = query * BF16(0.125)
        for pair in range(pairs):
            queries[pair] = query[:, pair * 128 : pair * 128 + 128].reshape(times, block, 128)
        keep_rows(0, tokens)

    def project_rest(indices):
        taps = prepare(numbers[indices[0]])
        for at, index in enumerate(indices):
            tokens = project(index, taps)
            if at + 1 < len(indices):
                taps = prepare(numbers[indices[at + 1]])
            keep_rows(index, tokens)

    def project_or_clear(index):
        pl.when(count > index)(lambda: project_rest([index]))

        @pl.when(count <= index)
        def _():
            for pair in range(pairs):
                keys[pair, index] = jnp.zeros((times * block, 128), BF16)
                values[pair, index] = jnp.zeros((times * block, 128), BF16)

    for move in close + distant:
        shift(*move, "pass")
    for load in loads[:3]:
        load.wait()
    for move in close:
        shift(*move, "take")
    project_own()
    if flat:

        @pl.when(count == most)
        def _():
            project_rest([1])

        for move in distant:
            shift(*move, "take")

        @pl.when(count == most)
        def _():
            project_rest(range(2, most))

        @pl.when(count < most)
        def _():
            project_rest(range(1, most - 1))
    else:
        for move in distant:
            shift(*move, "take")
        for index in range(1, most):
            project_or_clear(index)

    biases = []
    for index, number in enumerate(numbers):
        listed = neighbours_ref[chan, 0] == number
        for entry in range(1, neighbours_ref.shape[1]):
            listed = listed | (neighbours_ref[chan, entry] == number)
        listed = listed & (count > index)
        biases.append(jnp.where(listed, 0.0, -jnp.inf).astype(F32))

    batch = heads
    span = batch * block
    half = lax.broadcasted_iota(jnp.int32, (span, 128), 1) < HEAD_SIZE

    ones = jnp.ones((times * block, 128), BF16)
    span = block
    half = lax.broadcasted_iota(jnp.int32, (span, 128), 1) < HEAD_SIZE

    def attend(chunk, held):
        units = [(time, pair) for time in range(heads) for pair in range(pairs)]

        def stack(unit):
            time, pair = unit
            both = queries[pair, chunk * heads + time]
            blank = jnp.zeros_like(both)
            return jnp.concatenate(
                [jnp.where(half, both, blank), jnp.where(half, blank, both)], axis=0
            )

        def score(query, pair, number):
            return lax.dot_general(
                query, keys[pair, number], NT_DIMS, preferred_element_type=F32
            )

        query = stack(units[0])
        ahead = [score(query, units[0][1], number) for number in range(held)]
        for at, (time, pair) in enumerate(units):
            scores, ahead = ahead, []
            tops = [
                jnp.max(scores[number], axis=1, keepdims=True) + biases[number]
                for number in range(held)
            ]
            peak = functools.reduce(jnp.maximum, tops)
            if at + 1 < len(units):
                query = stack(units[at + 1])
            output = None
            for number in range(held):
                if at + 1 < len(units):
                    ahead.append(score(query, units[at + 1][1], number))
                weights = jnp.exp(scores[number] - (peak - biases[number])).astype(BF16)
                value = jnp.concatenate([values[pair, number], ones], axis=1)
                part = jnp.dot(weights, value, preferred_element_type=F32)
                output = part if output is None else output + part
            result = output[:, :128] / output[:, 128:]
            attended[chunk * heads + time, pair] = jnp.where(
                half, result[:span], result[span:]
            ).astype(BF16)

    counts = (most - 1, most) if flat else (most,)
    swaps = []
    for far in range(1, tms + 1):
        chunk = lax.rem(tm + far, tms)
        for held in counts:

            def each(held=held):
                attend(chunk, held)

            if len(counts) == 1:
                each()
            else:
                pl.when(count == held)(each)
        for step in range(0 if far < tms else 1, heads):
            to_head = lax.rem(head + step, heads)
            swaps.append(
                send(
                    attended.at[chunk * heads + to_head],
                    received.at[group],
                    swap_sems,
                    far % tms * heads + step,
                    {"tm": chunk, "head": to_head},
                )
            )
    def exchange(buffer, near, sems):
        copies = []
        for number, (far, step) in enumerate(near):
            copies.append(send(buffer, buffer, sems, number, device(far, step)))
        return copies

    for pair in range(pairs):
        part = attended[:, pair].reshape(times * block, 128).astype(F32)
        sums[chan, group, pair] = jnp.sum(part, axis=0, keepdims=True)
        lanes = pl.ds(pl.multiple_of(column + pair * 128, 128), 128)
        part = tokens_own[:, :, lanes].reshape(times * block, 128).astype(F32)
        sums[chan, group, pairs + pair] = jnp.sum(part, axis=0, keepdims=True)
    if flat:
        near = sorted(peers, key=lambda pair: -pair[0] * (chans - pair[0]))
    else:
        near = [pair for pair in peers if pair[0] == 0]
    totals = exchange(sums.at[chan, group], near, sum_sems)
    received[group] = attended[group]
    for load in loads[3:]:
        load.wait()
    for copy in swaps:
        copy.wait_recv()
    merged = jnp.concatenate(
        [received[time, pair] for time in range(times) for pair in range(pairs)], axis=1
    )
    branch = jnp.dot(merged, w_out[...], preferred_element_type=F32)
    encoded_ref[...] = (tokens_own[group].astype(F32) + branch).astype(BF16)
    write = pltpu.make_async_copy(encoded_ref, encoded_hbm, w_sem.at[12])
    write.start()

    seismo = seismo_ref[...]
    unit = seismo / jnp.sqrt(jnp.sum(seismo * seismo, axis=1, keepdims=True) + 1e-06)
    for copy in totals:
        copy.wait_recv()

    summed = range(chans) if flat else [chan]

    def assemble(first):
        rows = []
        for number in summed:
            parts = [sums[number, g, first + pair] for g in range(times) for pair in range(pairs)]
            rows.append(jnp.concatenate(parts, axis=1))
        return jnp.concatenate(rows, axis=0) / (times * block)

    mean = assemble(0)
    coarse = mean.astype(BF16)
    fine = (mean - coarse.astype(F32)).astype(BF16)
    mixed = jnp.dot(
        jnp.concatenate([coarse, fine], axis=0), w_out[...], preferred_element_type=F32
    )
    pooled = assemble(pairs) + mixed[: len(summed)] + mixed[len(summed) :]
    projected = jnp.dot(pooled.astype(BF16), w_pool[...], preferred_element_type=F32)
    every = projected / jnp.sqrt(
        jnp.sum(projected * projected, axis=1, keepdims=True) + 1e-06
    )
    if not flat:
        embeds[chan] = every
        near = [pair for pair in peers if pair[1] == 0]
        for copy in exchange(embeds.at[chan], near, embed_sems):
            copy.wait_recv()
        every = jnp.concatenate([embeds[number] for number in range(chans)], axis=0)
    logits = 50.0 * lax.dot_general(
        every, unit, NT_DIMS, precision=lax.Precision.HIGHEST, preferred_element_type=F32
    )
    spread = jnp.log(jnp.sum(jnp.exp(logits), axis=0, keepdims=True))
    matches = lax.broadcasted_iota(jnp.int32, logits.shape, 0) == colocated_ref[...]
    label = jnp.sum(jnp.where(matches, logits, 0.0), axis=0, keepdims=True)
    loss_ref[...] = spread - label
    store = pltpu.make_async_copy(loss_ref, loss_hbm, w_sem.at[13])
    store.start()
    write.wait()
    store.wait()
    for move in moves:
        shift(*move, "end")
    for copy in started:
        copy.wait_send()


def hand_over(encoded_ref, loss_ref, encoded_out, loss_out):
    encoded_out[...] = encoded_ref[...]
    loss_out[...] = loss_ref[...]


def on_device(
    strain, stem_weight, attn_in, attn_out, pool_weight, neighbours, seismo_embed, colocated
):
    chans, tms, heads = (lax.axis_size(axis) for axis in ("chan", "tm", "head"))
    times = tms * heads
    width = attn_in.shape[0]
    slab = width // times
    pairs = slab // 128
    block = strain.shape[1] // PC
    reach = 2 if chans <= 4 else 3
    own = reach + 1
    gathered = 2 * own + 1
    most = min(2 * reach + 1, chans)
    place, pick = tap_tables()
    vmem = pl.BlockSpec(memory_space=pltpu.VMEM)
    hbm = pl.BlockSpec(memory_space=pl.ANY)
    dma = pltpu.SemaphoreType.DMA
    sizes = (chans, tms, heads, block, slab, width, own, most)
    shapes = (
        jax.ShapeDtypeStruct((block, width), BF16),
        jax.ShapeDtypeStruct((1, seismo_embed.shape[0]), F32),
    )
    encoded, loss = pl.pallas_call(
        functools.partial(layer, sizes),
        out_shape=shapes,
        in_specs=[hbm] * 10,
        out_specs=(hbm, hbm),
        scratch_shapes=[
            pltpu.VMEM((times, gathered, block, 128), BF16),
            pltpu.VMEM((times, block, width), BF16),
            pltpu.VMEM((pairs, times, block, 128), BF16),
            pltpu.VMEM((pairs, most, times * block, 128), BF16),
            pltpu.VMEM((pairs, most, times * block, 128), BF16),
            pltpu.VMEM((times, pairs, block, 128), BF16),
            pltpu.VMEM((times, pairs, block, 128), BF16),
            pltpu.VMEM((chans, times, 2 * pairs, 1, 128), F32),
            pltpu.VMEM((chans, 1, pool_weight.shape[1]), F32),
            pltpu.VMEM((width, slab), BF16),
            pltpu.VMEM((width, slab), BF16),
            pltpu.VMEM((width, slab), BF16),
            pltpu.VMEM(attn_out.shape, BF16),
            pltpu.VMEM(pool_weight.shape, BF16),
            pltpu.VMEM(strain.shape, BF16),
            pltpu.VMEM(stem_weight.shape, BF16),
            pltpu.VMEM((256, width), BF16),
            pltpu.VMEM(place.shape, BF16),
            pltpu.VMEM(pick.shape, BF16),
            pltpu.VMEM(seismo_embed.shape, F32),
            pltpu.VMEM((1, seismo_embed.shape[0]), jnp.int32),
            pltpu.VMEM((block, width), BF16),
            pltpu.VMEM((1, seismo_embed.shape[0]), F32),
            pltpu.SMEM(neighbours.shape, jnp.int32),
            dma((14,)),
            pltpu.SemaphoreType.REGULAR((2, chans)),
            dma((2, tms * gathered)),
            dma((2, tms * gathered * heads)),
            dma((2, times)),
            dma((2, chans * times)),
            dma((2, chans)),
        ],
        compiler_params=pltpu.CompilerParams(
            collective_id=0, has_side_effects=True, vmem_limit_bytes=56 * 1024 * 1024
        ),
    )(
        strain,
        stem_weight,
        attn_in,
        attn_out,
        pool_weight,
        jnp.asarray(place, BF16),
        jnp.asarray(pick, BF16),
        neighbours,
        seismo_embed,
        colocated[None, :],
    )
    encoded, loss = pl.pallas_call(
        hand_over,
        out_shape=shapes,
        in_specs=[vmem, vmem],
        out_specs=(vmem, vmem),
    )(encoded, loss)
    return (encoded[None], loss[0])


def solution(mesh):
    in_specs = (
        P(("grp", "tm", "head"), "chan"),
        P(),
        P(),
        P(),
        P(),
        P("grp", None),
        P("grp", None),
        P("grp"),
    )
    out_specs = (P(("grp", "tm", "head"), "chan", None), P("grp"))
    return jax.shard_map(
        on_device, mesh=mesh, in_specs=in_specs, out_specs=out_specs, check_vma=False
    )
```

```python
import functools

import jax
import jax.numpy as jnp
import numpy as np
from jax import lax
from jax.experimental import pallas as pl
from jax.experimental.pallas import tpu as pltpu
from jax.sharding import PartitionSpec as P

HEAD_SIZE = 64
PC = 8
PT = 16
EDGE = 16
MESH = pl.DeviceIdType.MESH
F32 = jnp.float32
BF16 = jnp.bfloat16
NT_DIMS = (((1,), (1,)), ((), ()))


def tap_tables():
    place = np.zeros((256, (PT + 2) * (PC + 2)), np.float32)
    pick = np.zeros((128, 128), np.float32)
    tap = lambda i, j: (i + 1) * (PC + 2) + j + 1
    lane = lambda i, j: j * PT + i
    for i in range(PT):
        for j in range(PC):
            place[lane(i, j), tap(i, j)] = 1
        place[128 + 112 + i, tap(i, -1)] = 1
        place[128 + i, tap(i, PC)] = 1
    for j in range(PC):
        place[128 + 16 + j, tap(-1, j)] = 1
        place[128 + 32 + j, tap(PT, j)] = 1
        pick[lane(PT - 1, j), 16 + j] = 1
        pick[lane(0, j), 32 + j] = 1
    corners = ((48, -1, -1), (49, -1, PC), (50, PT, -1), (51, PT, PC))
    for at, i, j in corners:
        place[128 + at, tap(i, j)] = 1
        pick[lane(i % PT, j % PC), at] = 1
    return place, pick


def layer(
    sizes,
    strain_hbm,
    stem_hbm,
    attn_in_ref,
    attn_out_ref,
    pool_ref,
    place_hbm,
    pick_hbm,
    neighbours_hbm,
    seismo_hbm,
    colocated_hbm,
    encoded_hbm,
    loss_hbm,
    tiles,
    tokens_own,
    queries,
    keys,
    values,
    attended,
    received,
    sums,
    embeds,
    w_query,
    w_key,
    w_value,
    w_out,
    w_pool,
    strain_ref,
    raw_ref,
    stem_ref,
    place_ref,
    pick_ref,
    seismo_ref,
    colocated_ref,
    encoded_ref,
    loss_ref,
    neighbours_ref,
    w_sem,
    far_sems,
    tile_sems,
    head_sems,
    swap_sems,
    sum_sems,
    embed_sems,
):
    chans, tms, heads, block, slab, width, own, most = sizes
    times = tms * heads
    pairs = slab // 128
    reach = own - 1
    chan = lax.axis_index("chan")
    tm = lax.axis_index("tm")
    head = lax.axis_index("head")
    group = tm * heads + head

    barrier = pltpu.get_barrier_semaphore()
    flat = chans * times <= 16
    peers = [(far, step) for far in range(chans) for step in range(times)]
    peers = [
        pair
        for pair in peers
        if any(pair)
        and (flat or not all(pair) or (pair[1] % heads == 0 and min(pair[0], chans - pair[0]) <= own))
    ]

    peers = sorted(peers, key=lambda pair: -min(pair[0], chans - pair[0]))

    def device(far, step):
        peer = lax.rem(group + step, times)
        return {
            "chan": lax.rem(chan + far, chans),
            "tm": peer // heads,
            "head": lax.rem(peer, heads),
        }

    def greet(far):
        for step in range(times):
            if far or step:
                peer = lax.rem(group + step, times)
                target = {"chan": chan + far, "tm": peer // heads, "head": lax.rem(peer, heads)}
                pl.semaphore_signal(barrier, inc=1, device_id=target, device_id_type=MESH)

    below, above = chan > 0, chan < chans - 1
    if flat:
        greet(0)
        pl.when(below)(lambda: greet(-1))
        pl.when(above)(lambda: greet(1))
    else:
        for far, step in peers:
            pl.semaphore_signal(barrier, inc=1, device_id=device(far, step), device_id_type=MESH)

    first = pltpu.make_async_copy(strain_hbm, strain_ref, w_sem.at[5])
    first.start()
    small = []
    for number, (source, buffer) in enumerate(
        (
            (stem_hbm, raw_ref),
            (place_hbm, place_ref),
            (pick_hbm, pick_ref),
            (neighbours_hbm, neighbours_ref),
            (seismo_hbm, seismo_ref),
            (colocated_hbm, colocated_ref),
        )
    ):
        small.append(pltpu.make_async_copy(source, buffer, w_sem.at[6 + number]))
        small[-1].start()
    column = pl.multiple_of(group * slab, slab)
    loads = []
    for number, buffer in enumerate((w_query, w_key, w_value)):
        source = attn_in_ref.at[:, pl.ds(number * width + column, slab)]
        loads.append(pltpu.make_async_copy(source, buffer, w_sem.at[number]))
    loads.append(pltpu.make_async_copy(attn_out_ref, w_out, w_sem.at[3]))
    loads.append(pltpu.make_async_copy(pool_ref, w_pool, w_sem.at[4]))
    for load in loads:
        load.start()

    lanes16 = lax.broadcasted_iota(jnp.int32, (PT, 128), 1)
    rows16 = lax.broadcasted_iota(jnp.int32, (PT, 128), 0)
    spread_eye = jnp.where(lax.rem(lanes16, PT) == rows16, 1.0, 0.0).astype(BF16)
    first.wait()
    spread = lax.dot_general(
        strain_ref[...], spread_eye, (((0,), (0,)), ((), ())), preferred_element_type=F32
    )
    sample = lax.rem(lax.broadcasted_iota(jnp.int32, spread.shape, 0), PC)
    slot = lax.broadcasted_iota(jnp.int32, spread.shape, 1) // PT
    spread = jnp.where(sample == slot, spread, 0.0)
    tiles[group, own] = jnp.sum(spread.reshape(block, PC, 128), axis=1).astype(BF16)

    for load in small:
        load.wait()
    stem_ref[...] = jnp.dot(
        place_ref[...], raw_ref[...], preferred_element_type=F32
    ).astype(BF16)

    def tell(sem, far):
        pl.semaphore_signal(sem, inc=1, device_id={"chan": chan + far}, device_id_type=MESH)

    def learn(hop):
        pl.when(chan >= hop)(lambda: pl.semaphore_wait(far_sems.at[0, hop - 2], 1))
        pl.when(chan + hop < chans)(lambda: pl.semaphore_wait(far_sems.at[1, hop - 2], 1))

    if flat:
        sides = jnp.where(below, times, 0) + jnp.where(above, times, 0)
        pl.semaphore_wait(barrier, times - 1 + sides)
    else:
        pl.semaphore_wait(barrier, len(peers))

    started = []

    def send(source, target, sems, number, device):
        copy = pltpu.make_async_remote_copy(
            src_ref=source,
            dst_ref=target,
            send_sem=sems.at[0, number],
            recv_sem=sems.at[1, number],
            device_id=device,
            device_id_type=MESH,
        )
        copy.start()
        started.append(copy)
        return copy

    def shift(far, step, start):
        number = (far + own) * tms + step

        def tile(time_row):
            place = own - far
            if far == own:
                return tiles.at[time_row, place, pl.ds(block - EDGE, EDGE)]
            if far == -own:
                return tiles.at[time_row, place, pl.ds(0, EDGE)]
            return tiles.at[time_row, place]

        def outward():
            source = tiles.at[group, own]
            if abs(far) == own:
                source = tiles.at[group, own, pl.ds(block - EDGE if far > 0 else 0, EDGE)]
            return pltpu.make_async_remote_copy(
                src_ref=source,
                dst_ref=tile(group),
                send_sem=tile_sems.at[0, number],
                recv_sem=tile_sems.at[1, number],
                device_id={"chan": chan + far, "tm": lax.rem(tm + step, tms)},
                device_id_type=MESH,
            )

        def inward(from_step):
            row = lax.rem(tm + tms - step, tms) * heads + head
            return pltpu.make_async_remote_copy(
                src_ref=tile(row),
                dst_ref=tile(row),
                send_sem=head_sems.at[0, number * heads + from_step],
                recv_sem=head_sems.at[1, number * heads + from_step],
                device_id={"head": lax.rem(head + from_step, heads)},
                device_id_type=MESH,
            )

        here = (chan + far >= 0) & (chan + far < chans)
        there = (chan - far >= 0) & (chan - far < chans)
        local = far == 0 and step == 0

        def run(when, action):
            if far == 0:
                action()
            else:
                pl.when(when)(action)

        if start == "send" and not local:
            run(here, lambda: outward().start())
        if start == "pass":

            def relay():
                if not local:
                    outward().wait_recv()
                for from_step in range(1, heads):
                    inward(from_step).start()

            run(there, relay)
        if start == "take":

            def take():
                for from_step in range(1, heads):
                    inward(from_step).wait_recv()

            run(there, take)
        if start == "end":
            if not local:
                run(here, lambda: outward().wait_send())

            def done():
                for from_step in range(1, heads):
                    inward(from_step).wait_send()

            run(there, done)

    moves = [(far, step) for far in range(-own, own + 1) for step in range(tms)]
    moves = sorted(moves, key=lambda move: abs(move[0]) + move[1])
    close = [move for move in moves if abs(move[0]) <= 1]
    distant = [move for move in moves if abs(move[0]) > 1]
    for move in close[::-1]:
        shift(*move, "send")
    for hop in range(2, own + 1):
        if flat:
            if hop > 2:
                learn(hop - 1)
                for move in distant:
                    if abs(move[0]) == hop - 1:
                        shift(*move, "send")
            if hop < chans:
                pl.when((chan >= hop - 1) & above)(lambda: tell(far_sems.at[0, hop - 2], 1))
                pl.when((chan + hop <= chans) & below)(lambda: tell(far_sems.at[1, hop - 2], -1))
    if flat:
        learn(own)
    for move in distant:
        if abs(move[0]) == own or not flat:
            shift(*move, "send")
    long = block + 2 * EDGE
    lane = lax.broadcasted_iota(jnp.int32, (long, 128), 1)
    toward = jnp.where(2 * chan < chans, -1, 1)
    numbers = [jnp.int32(0) * chan for _ in range(most)]
    count = jnp.int32(0) * chan
    for away in range(reach + 1):
        for side in (toward, -toward) if away else (toward,):
            number = chan + away * side
            valid = (number >= 0) & (number < chans)
            for index in range(most):
                numbers[index] = jnp.where(valid & (count == index), number, numbers[index])
            count = count + jnp.where(valid, 1, 0)

    def prepare(number):
        place = number - chan + own
        before = jnp.maximum(number - 1, 0) - chan + own
        after = jnp.minimum(number + 1, chans - 1) - chan + own
        has_before = jnp.where(number > 0, 1.0, 0.0)
        has_after = jnp.where(number < chans - 1, 1.0, 0.0)
        pieces, picks = [], []
        for time in range(times):
            head_rows = tiles[time, before, block - EDGE :]
            tail_rows = tiles[time, after, :EDGE]
            piece = jnp.concatenate([head_rows, tiles[time, place], tail_rows], axis=0)
            pieces.append(piece)
        picked = jnp.dot(
            jnp.concatenate(pieces, axis=0), pick_ref[...], preferred_element_type=F32
        )
        zeros = jnp.zeros((long, 128), F32)
        row = lax.broadcasted_iota(jnp.int32, (long, 128), 0)
        keep = jnp.where(row < EDGE, has_before, jnp.where(row >= EDGE + block, has_after, 1.0))
        taps = []
        for time in range(times):
            here32 = pieces[time].astype(F32)
            above = picked[(time - 1) * long : time * long] if time else zeros
            below = picked[(time + 1) * long : (time + 2) * long] if time < times - 1 else zeros
            left = jnp.where(
                lane >= 112, here32, jnp.where(lane == 48, above, jnp.where(lane == 50, below, 0.0))
            )
            right = jnp.where(
                lane < 16, here32, jnp.where(lane == 49, above, jnp.where(lane == 51, below, 0.0))
            )
            left = pltpu.roll(left * keep, 1, 0)[EDGE : EDGE + block]
            right = pltpu.roll(right * keep, long - 1, 0)[EDGE : EDGE + block]
            inner = lane[:block]
            middle = jnp.where(
                (inner >= 16) & (inner < 24),
                above[EDGE : EDGE + block],
                jnp.where((inner >= 32) & (inner < 40), below[EDGE : EDGE + block], 0.0),
            )
            halo = (left + right + middle).astype(BF16)
            taps.append(jnp.concatenate([pieces[time][EDGE : EDGE + block], halo], axis=1))
        return jnp.concatenate(taps, axis=0)

    def project(index, taps):
        return jnp.dot(taps, stem_ref[...], preferred_element_type=F32).astype(BF16)

    def keep_rows(index, tokens):
        key = jnp.dot(tokens, w_key[...], preferred_element_type=F32).astype(BF16)
        value = jnp.dot(tokens, w_value[...], preferred_element_type=F32).astype(BF16)
        for pair in range(pairs):
            part = slice(pair * 128, pair * 128 + 128)
            keys[pair, index] = key[:, part]
            values[pair, index] = value[:, part]

    def project_own():
        tokens = project(0, prepare(chan))
        tokens_own[...] = tokens.reshape(times, block, width)
        query = jnp.dot(tokens, w_query[...], preferred_element_type=F32).astype(BF16)
        query = query * BF16(0.125)
        for pair in range(pairs):
            queries[pair] = query[:, pair * 128 : pair * 128 + 128].reshape(times, block, 128)
        keep_rows(0, tokens)

    def project_rest(indices):
        taps = prepare(numbers[indices[0]])
        for at, index in enumerate(indices):
            tokens = project(index, taps)
            if at + 1 < len(indices):
                taps = prepare(numbers[indices[at + 1]])
            keep_rows(index, tokens)

    def project_or_clear(index):
        pl.when(count > index)(lambda: project_rest([index]))

        @pl.when(count <= index)
        def _():
            for pair in range(pairs):
                keys[pair, index] = jnp.zeros((times * block, 128), BF16)
                values[pair, index] = jnp.zeros((times * block, 128), BF16)

    for move in close + distant:
        shift(*move, "pass")
    for load in loads[:3]:
        load.wait()
    for move in close:
        shift(*move, "take")
    project_own()
    own_tokens = tokens_own[group].astype(F32)
    sums[chan, group] = jnp.sum(own_tokens, axis=0, keepdims=True)
    if flat:

        @pl.when(count == most)
        def _():
            project_rest([1])

        for move in distant:
            shift(*move, "take")

        @pl.when(count == most)
        def _():
            project_rest(range(2, most))

        @pl.when(count < most)
        def _():
            project_rest(range(1, most - 1))
    else:
        for move in distant:
            shift(*move, "take")
        for index in range(1, most):
            project_or_clear(index)

    biases = []
    for index, number in enumerate(numbers):
        listed = neighbours_ref[chan, 0] == number
        for entry in range(1, neighbours_ref.shape[1]):
            listed = listed | (neighbours_ref[chan, entry] == number)
        listed = listed & (count > index)
        biases.append(jnp.where(listed, 0.0, -jnp.inf).astype(F32))

    batch = heads
    span = batch * block
    half = lax.broadcasted_iota(jnp.int32, (span, 128), 1) < HEAD_SIZE

    ones = jnp.ones((times * block, 128), BF16)
    span = block
    half = lax.broadcasted_iota(jnp.int32, (span, 128), 1) < HEAD_SIZE

    def attend(chunk, held):
        units = [(time, pair) for time in range(heads) for pair in range(pairs)]

        def stack(unit):
            time, pair = unit
            both = queries[pair, chunk * heads + time]
            blank = jnp.zeros_like(both)
            return jnp.concatenate(
                [jnp.where(half, both, blank), jnp.where(half, blank, both)], axis=0
            )

        def score(query, pair, number):
            return lax.dot_general(
                query, keys[pair, number], NT_DIMS, preferred_element_type=F32
            )

        query = stack(units[0])
        ahead = [score(query, units[0][1], number) for number in range(held)]
        for at, (time, pair) in enumerate(units):
            scores, ahead = ahead, []
            tops = [
                jnp.max(scores[number], axis=1, keepdims=True) + biases[number]
                for number in range(held)
            ]
            peak = functools.reduce(jnp.maximum, tops)
            if at + 1 < len(units):
                query = stack(units[at + 1])
            output = None
            for number in range(held):
                if at + 1 < len(units):
                    ahead.append(score(query, units[at + 1][1], number))
                weights = jnp.exp(scores[number] - (peak - biases[number])).astype(BF16)
                value = jnp.concatenate([values[pair, number], ones], axis=1)
                part = jnp.dot(weights, value, preferred_element_type=F32)
                output = part if output is None else output + part
            result = output[:, :128] / output[:, 128:]
            attended[chunk * heads + time, pair] = jnp.where(
                half, result[:span], result[span:]
            ).astype(BF16)

    counts = (most - 1, most) if flat else (most,)
    swaps = []
    for far in range(1, tms + 1):
        chunk = lax.rem(tm + far, tms)
        for held in counts:

            def each(held=held):
                attend(chunk, held)

            if len(counts) == 1:
                each()
            else:
                pl.when(count == held)(each)
        for step in range(0 if far < tms else 1, heads):
            to_head = lax.rem(head + step, heads)
            swaps.append(
                send(
                    attended.at[chunk * heads + to_head],
                    received.at[group],
                    swap_sems,
                    far % tms * heads + step,
                    {"tm": chunk, "head": to_head},
                )
            )
    def exchange(buffer, near, sems):
        copies = []
        for number, (far, step) in enumerate(near):
            copies.append(send(buffer, buffer, sems, number, device(far, step)))
        return copies

    for load in loads[3:]:
        load.wait()
    parts = []
    for pair in range(pairs):
        part = attended[:, pair].reshape(times * block, 128).astype(F32)
        parts.append(jnp.sum(part, axis=0, keepdims=True))
    part = jnp.concatenate(parts, axis=1)
    coarse = part.astype(BF16)
    fine = (part - coarse.astype(F32)).astype(BF16)
    mixed = jnp.dot(
        jnp.concatenate([coarse, fine], axis=0),
        w_out[pl.ds(column, slab), :],
        preferred_element_type=F32,
    )
    sums[chan, group] = sums[chan, group] + mixed[:1] + mixed[1:]
    if flat:
        near = sorted(peers, key=lambda pair: -pair[0])
    else:
        near = [pair for pair in peers if pair[0] == 0]
    totals = exchange(sums.at[chan, group], near, sum_sems)
    received[group] = attended[group]
    for copy in swaps:
        copy.wait_recv()
    merged = jnp.concatenate(
        [received[time, pair] for time in range(times) for pair in range(pairs)], axis=1
    )
    branch = jnp.dot(merged, w_out[...], preferred_element_type=F32)
    encoded_ref[...] = (tokens_own[group].astype(F32) + branch).astype(BF16)
    write = pltpu.make_async_copy(encoded_ref, encoded_hbm, w_sem.at[12])
    write.start()

    seismo = seismo_ref[...]
    unit = seismo / jnp.sqrt(jnp.sum(seismo * seismo, axis=1, keepdims=True) + 1e-06)
    unit_coarse = unit.astype(BF16)
    unit_fine = (unit - unit_coarse.astype(F32)).astype(BF16)
    for move in moves:
        shift(*move, "end")
    for copy in swaps:
        copy.wait_send()
    for copy in totals:
        copy.wait_recv()

    summed = range(chans) if flat else [chan]

    def pool(number):
        pooled = sums[number, 0]
        for time in range(1, times):
            pooled = pooled + sums[number, time]
        return pooled / (times * block)

    pooled = jnp.concatenate([pool(number) for number in summed], axis=0)
    projected = jnp.dot(pooled.astype(BF16), w_pool[...], preferred_element_type=F32)
    every = projected * lax.rsqrt(
        jnp.sum(projected * projected, axis=1, keepdims=True) + 1e-06
    )
    if not flat:
        embeds[chan] = every
        near = [pair for pair in peers if pair[1] == 0]
        for copy in exchange(embeds.at[chan], near, embed_sems):
            copy.wait_recv()
        every = jnp.concatenate([embeds[number] for number in range(chans)], axis=0)
    every_coarse = every.astype(BF16)
    every_fine = (every - every_coarse.astype(F32)).astype(BF16)
    logits = 50.0 * lax.dot_general(
        jnp.concatenate([every_coarse, every_fine, every_coarse], axis=1),
        jnp.concatenate([unit_coarse, unit_coarse, unit_fine], axis=1),
        NT_DIMS,
        preferred_element_type=F32,
    )
    spread = jnp.log(jnp.sum(jnp.exp(logits), axis=0, keepdims=True))
    matches = lax.broadcasted_iota(jnp.int32, logits.shape, 0) == colocated_ref[...]
    label = jnp.sum(jnp.where(matches, logits, 0.0), axis=0, keepdims=True)
    loss_ref[...] = spread - label
    store = pltpu.make_async_copy(loss_ref, loss_hbm, w_sem.at[13])
    store.start()
    write.wait()
    store.wait()
    for copy in started[len(swaps) :]:
        copy.wait_send()


def hand_over(encoded_ref, loss_ref, encoded_out, loss_out):
    encoded_out[...] = encoded_ref[...]
    loss_out[...] = loss_ref[...]


def on_device(
    strain, stem_weight, attn_in, attn_out, pool_weight, neighbours, seismo_embed, colocated
):
    chans, tms, heads = (lax.axis_size(axis) for axis in ("chan", "tm", "head"))
    times = tms * heads
    width = attn_in.shape[0]
    slab = width // times
    pairs = slab // 128
    block = strain.shape[1] // PC
    reach = 2 if chans <= 4 else 3
    own = reach + 1
    gathered = 2 * own + 1
    most = min(2 * reach + 1, chans)
    place, pick = tap_tables()
    vmem = pl.BlockSpec(memory_space=pltpu.VMEM)
    hbm = pl.BlockSpec(memory_space=pl.ANY)
    dma = pltpu.SemaphoreType.DMA
    sizes = (chans, tms, heads, block, slab, width, own, most)
    shapes = (
        jax.ShapeDtypeStruct((block, width), BF16),
        jax.ShapeDtypeStruct((1, seismo_embed.shape[0]), F32),
    )
    encoded, loss = pl.pallas_call(
        functools.partial(layer, sizes),
        out_shape=shapes,
        in_specs=[hbm] * 10,
        out_specs=(hbm, hbm),
        scratch_shapes=[
            pltpu.VMEM((times, gathered, block, 128), BF16),
            pltpu.VMEM((times, block, width), BF16),
            pltpu.VMEM((pairs, times, block, 128), BF16),
            pltpu.VMEM((pairs, most, times * block, 128), BF16),
            pltpu.VMEM((pairs, most, times * block, 128), BF16),
            pltpu.VMEM((times, pairs, block, 128), BF16),
            pltpu.VMEM((times, pairs, block, 128), BF16),
            pltpu.VMEM((chans, times, 1, width), F32),
            pltpu.VMEM((chans, 1, pool_weight.shape[1]), F32),
            pltpu.VMEM((width, slab), BF16),
            pltpu.VMEM((width, slab), BF16),
            pltpu.VMEM((width, slab), BF16),
            pltpu.VMEM(attn_out.shape, BF16),
            pltpu.VMEM(pool_weight.shape, BF16),
            pltpu.VMEM(strain.shape, BF16),
            pltpu.VMEM(stem_weight.shape, BF16),
            pltpu.VMEM((256, width), BF16),
            pltpu.VMEM(place.shape, BF16),
            pltpu.VMEM(pick.shape, BF16),
            pltpu.VMEM(seismo_embed.shape, F32),
            pltpu.VMEM((1, seismo_embed.shape[0]), jnp.int32),
            pltpu.VMEM((block, width), BF16),
            pltpu.VMEM((1, seismo_embed.shape[0]), F32),
            pltpu.SMEM(neighbours.shape, jnp.int32),
            dma((14,)),
            pltpu.SemaphoreType.REGULAR((2, chans)),
            dma((2, tms * gathered)),
            dma((2, tms * gathered * heads)),
            dma((2, times)),
            dma((2, chans * times)),
            dma((2, chans)),
        ],
        compiler_params=pltpu.CompilerParams(
            collective_id=0, has_side_effects=True, vmem_limit_bytes=56 * 1024 * 1024
        ),
    )(
        strain,
        stem_weight,
        attn_in,
        attn_out,
        pool_weight,
        jnp.asarray(place, BF16),
        jnp.asarray(pick, BF16),
        neighbours,
        seismo_embed,
        colocated[None, :],
    )
    encoded, loss = pl.pallas_call(
        hand_over,
        out_shape=shapes,
        in_specs=[vmem, vmem],
        out_specs=(vmem, vmem),
    )(encoded, loss)
    return (encoded[None], loss[0])


def solution(mesh):
    in_specs = (
        P(("grp", "tm", "head"), "chan"),
        P(),
        P(),
        P(),
        P(),
        P("grp", None),
        P("grp", None),
        P("grp"),
    )
    out_specs = (P(("grp", "tm", "head"), "chan", None), P("grp"))
    return jax.shard_map(
        on_device, mesh=mesh, in_specs=in_specs, out_specs=out_specs, check_vma=False
    )
```

```python
import functools

import jax
import jax.numpy as jnp
import numpy as np
from jax import lax
from jax.experimental import pallas as pl
from jax.experimental.pallas import tpu as pltpu
from jax.sharding import PartitionSpec as P

HEAD_SIZE = 64
PC = 8
PT = 16
EDGE = 16
MESH = pl.DeviceIdType.MESH
F32 = jnp.float32
BF16 = jnp.bfloat16
NT_DIMS = (((1,), (1,)), ((), ()))


def tap_tables():
    place = np.zeros((256, (PT + 2) * (PC + 2)), np.float32)
    pick = np.zeros((128, 128), np.float32)
    tap = lambda i, j: (i + 1) * (PC + 2) + j + 1
    lane = lambda i, j: j * PT + i
    for i in range(PT):
        for j in range(PC):
            place[lane(i, j), tap(i, j)] = 1
        place[128 + 112 + i, tap(i, -1)] = 1
        place[128 + i, tap(i, PC)] = 1
    for j in range(PC):
        place[128 + 16 + j, tap(-1, j)] = 1
        place[128 + 32 + j, tap(PT, j)] = 1
        pick[lane(PT - 1, j), 16 + j] = 1
        pick[lane(0, j), 32 + j] = 1
    corners = ((48, -1, -1), (49, -1, PC), (50, PT, -1), (51, PT, PC))
    for at, i, j in corners:
        place[128 + at, tap(i, j)] = 1
        pick[lane(i % PT, j % PC), at] = 1
    return place, pick


def layer(
    sizes,
    strain_hbm,
    stem_hbm,
    attn_in_ref,
    attn_out_ref,
    pool_ref,
    place_hbm,
    pick_hbm,
    neighbours_hbm,
    seismo_hbm,
    colocated_hbm,
    encoded_hbm,
    loss_hbm,
    tiles,
    tokens_own,
    queries,
    keys,
    values,
    attended,
    received,
    sums,
    embeds,
    w_query,
    w_key,
    w_value,
    w_out,
    w_pool,
    strain_ref,
    raw_ref,
    stem_ref,
    place_ref,
    pick_ref,
    seismo_ref,
    colocated_ref,
    encoded_ref,
    loss_ref,
    neighbours_ref,
    w_sem,
    far_sems,
    tile_sems,
    head_sems,
    swap_sems,
    sum_sems,
    embed_sems,
):
    chans, tms, heads, block, slab, width, own, most = sizes
    times = tms * heads
    pairs = slab // 128
    reach = own - 1
    chan = lax.axis_index("chan")
    tm = lax.axis_index("tm")
    head = lax.axis_index("head")
    group = tm * heads + head

    barrier = pltpu.get_barrier_semaphore()
    flat = chans * times <= 16
    peers = [(far, step) for far in range(chans) for step in range(times)]
    peers = [
        pair
        for pair in peers
        if any(pair)
        and (flat or not all(pair) or (pair[1] % heads == 0 and min(pair[0], chans - pair[0]) <= own))
    ]

    peers = sorted(peers, key=lambda pair: -min(pair[0], chans - pair[0]))

    def device(far, step):
        peer = lax.rem(group + step, times)
        return {
            "chan": lax.rem(chan + far, chans),
            "tm": peer // heads,
            "head": lax.rem(peer, heads),
        }

    def greet(far):
        for step in range(times):
            if far or step:
                peer = lax.rem(group + step, times)
                target = {"chan": chan + far, "tm": peer // heads, "head": lax.rem(peer, heads)}
                pl.semaphore_signal(barrier, inc=1, device_id=target, device_id_type=MESH)

    below, above = chan > 0, chan < chans - 1
    if flat:
        greet(0)
        pl.when(below)(lambda: greet(-1))
        pl.when(above)(lambda: greet(1))
    else:
        for far, step in peers:
            pl.semaphore_signal(barrier, inc=1, device_id=device(far, step), device_id_type=MESH)

    first = pltpu.make_async_copy(strain_hbm, strain_ref, w_sem.at[5])
    first.start()
    small = []
    for number, (source, buffer) in enumerate(
        (
            (stem_hbm, raw_ref),
            (place_hbm, place_ref),
            (pick_hbm, pick_ref),
            (neighbours_hbm, neighbours_ref),
            (seismo_hbm, seismo_ref),
            (colocated_hbm, colocated_ref),
        )
    ):
        small.append(pltpu.make_async_copy(source, buffer, w_sem.at[6 + number]))
        small[-1].start()
    column = pl.multiple_of(group * slab, slab)
    loads = []
    for number, buffer in enumerate((w_query, w_key, w_value)):
        source = attn_in_ref.at[:, pl.ds(number * width + column, slab)]
        loads.append(pltpu.make_async_copy(source, buffer, w_sem.at[number]))
    loads.append(pltpu.make_async_copy(attn_out_ref, w_out, w_sem.at[3]))
    loads.append(pltpu.make_async_copy(pool_ref, w_pool, w_sem.at[4]))
    for load in loads:
        load.start()

    lanes16 = lax.broadcasted_iota(jnp.int32, (PT, 128), 1)
    rows16 = lax.broadcasted_iota(jnp.int32, (PT, 128), 0)
    spread_eye = jnp.where(lax.rem(lanes16, PT) == rows16, 1.0, 0.0).astype(BF16)
    first.wait()
    spread = lax.dot_general(
        strain_ref[...], spread_eye, (((0,), (0,)), ((), ())), preferred_element_type=F32
    )
    sample = lax.rem(lax.broadcasted_iota(jnp.int32, spread.shape, 0), PC)
    slot = lax.broadcasted_iota(jnp.int32, spread.shape, 1) // PT
    spread = jnp.where(sample == slot, spread, 0.0)
    tiles[group, own] = jnp.sum(spread.reshape(block, PC, 128), axis=1).astype(BF16)

    for load in small:
        load.wait()
    stem_ref[...] = jnp.dot(
        place_ref[...], raw_ref[...], preferred_element_type=F32
    ).astype(BF16)

    def tell(sem, far):
        pl.semaphore_signal(sem, inc=1, device_id={"chan": chan + far}, device_id_type=MESH)

    def learn(hop):
        pl.when(chan >= hop)(lambda: pl.semaphore_wait(far_sems.at[0, hop - 2], 1))
        pl.when(chan + hop < chans)(lambda: pl.semaphore_wait(far_sems.at[1, hop - 2], 1))

    if flat:
        sides = jnp.where(below, times, 0) + jnp.where(above, times, 0)
        pl.semaphore_wait(barrier, times - 1 + sides)
    else:
        pl.semaphore_wait(barrier, len(peers))

    started = []

    def send(source, target, sems, number, device):
        copy = pltpu.make_async_remote_copy(
            src_ref=source,
            dst_ref=target,
            send_sem=sems.at[0, number],
            recv_sem=sems.at[1, number],
            device_id=device,
            device_id_type=MESH,
        )
        copy.start()
        started.append(copy)
        return copy

    def shift(far, step, start):
        number = (far + own) * tms + step

        def tile(time_row):
            place = own - far
            if far == own:
                return tiles.at[time_row, place, pl.ds(block - EDGE, EDGE)]
            if far == -own:
                return tiles.at[time_row, place, pl.ds(0, EDGE)]
            return tiles.at[time_row, place]

        def outward():
            source = tiles.at[group, own]
            if abs(far) == own:
                source = tiles.at[group, own, pl.ds(block - EDGE if far > 0 else 0, EDGE)]
            return pltpu.make_async_remote_copy(
                src_ref=source,
                dst_ref=tile(group),
                send_sem=tile_sems.at[0, number],
                recv_sem=tile_sems.at[1, number],
                device_id={"chan": chan + far, "tm": lax.rem(tm + step, tms)},
                device_id_type=MESH,
            )

        def inward(from_step):
            row = lax.rem(tm + tms - step, tms) * heads + head
            return pltpu.make_async_remote_copy(
                src_ref=tile(row),
                dst_ref=tile(row),
                send_sem=head_sems.at[0, number * heads + from_step],
                recv_sem=head_sems.at[1, number * heads + from_step],
                device_id={"head": lax.rem(head + from_step, heads)},
                device_id_type=MESH,
            )

        here = (chan + far >= 0) & (chan + far < chans)
        there = (chan - far >= 0) & (chan - far < chans)
        local = far == 0 and step == 0

        def run(when, action):
            if far == 0:
                action()
            else:
                pl.when(when)(action)

        if start == "send" and not local:
            run(here, lambda: outward().start())
        if start == "pass":

            def relay():
                if not local:
                    outward().wait_recv()
                for from_step in range(1, heads):
                    inward(from_step).start()

            run(there, relay)
        if start == "take":

            def take():
                for from_step in range(1, heads):
                    inward(from_step).wait_recv()

            run(there, take)
        if start == "end":
            if not local:
                run(here, lambda: outward().wait_send())

            def done():
                for from_step in range(1, heads):
                    inward(from_step).wait_send()

            run(there, done)

    moves = [(far, step) for far in range(-own, own + 1) for step in range(tms)]
    moves = sorted(moves, key=lambda move: abs(move[0]) + move[1])
    close = [move for move in moves if abs(move[0]) <= 1]
    distant = [move for move in moves if abs(move[0]) > 1]
    for move in sorted(close, key=lambda move: (-move[1] * abs(move[0]), -abs(move[0]))):
        shift(*move, "send")
    shift(0, 0, "pass")
    for hop in range(2, own + 1):
        if flat:
            if hop > 2:
                learn(hop - 1)
                for move in distant:
                    if abs(move[0]) == hop - 1:
                        shift(*move, "send")
            if hop < chans:
                pl.when((chan >= hop - 1) & above)(lambda: tell(far_sems.at[0, hop - 2], 1))
                pl.when((chan + hop <= chans) & below)(lambda: tell(far_sems.at[1, hop - 2], -1))
    if flat:
        learn(own)
    for move in distant:
        if abs(move[0]) == own or not flat:
            shift(*move, "send")
    long = block + 2 * EDGE
    lane = lax.broadcasted_iota(jnp.int32, (long, 128), 1)
    toward = jnp.where(2 * chan < chans, -1, 1)
    numbers = [jnp.int32(0) * chan for _ in range(most)]
    count = jnp.int32(0) * chan
    for away in range(reach + 1):
        for side in (toward, -toward) if away else (toward,):
            number = chan + away * side
            valid = (number >= 0) & (number < chans)
            for index in range(most):
                numbers[index] = jnp.where(valid & (count == index), number, numbers[index])
            count = count + jnp.where(valid, 1, 0)

    def prepare(number):
        place = number - chan + own
        before = jnp.maximum(number - 1, 0) - chan + own
        after = jnp.minimum(number + 1, chans - 1) - chan + own
        has_before = jnp.where(number > 0, 1.0, 0.0)
        has_after = jnp.where(number < chans - 1, 1.0, 0.0)
        pieces, picks = [], []
        for time in range(times):
            head_rows = tiles[time, before, block - EDGE :]
            tail_rows = tiles[time, after, :EDGE]
            piece = jnp.concatenate([head_rows, tiles[time, place], tail_rows], axis=0)
            pieces.append(piece)
        picked = jnp.dot(
            jnp.concatenate(pieces, axis=0), pick_ref[...], preferred_element_type=F32
        )
        zeros = jnp.zeros((long, 128), F32)
        row = lax.broadcasted_iota(jnp.int32, (long, 128), 0)
        keep = jnp.where(row < EDGE, has_before, jnp.where(row >= EDGE + block, has_after, 1.0))
        taps = []
        for time in range(times):
            here32 = pieces[time].astype(F32)
            above = picked[(time - 1) * long : time * long] if time else zeros
            below = picked[(time + 1) * long : (time + 2) * long] if time < times - 1 else zeros
            left = jnp.where(
                lane >= 112, here32, jnp.where(lane == 48, above, jnp.where(lane == 50, below, 0.0))
            )
            right = jnp.where(
                lane < 16, here32, jnp.where(lane == 49, above, jnp.where(lane == 51, below, 0.0))
            )
            left = pltpu.roll(left * keep, 1, 0)[EDGE : EDGE + block]
            right = pltpu.roll(right * keep, long - 1, 0)[EDGE : EDGE + block]
            inner = lane[:block]
            middle = jnp.where(
                (inner >= 16) & (inner < 24),
                above[EDGE : EDGE + block],
                jnp.where((inner >= 32) & (inner < 40), below[EDGE : EDGE + block], 0.0),
            )
            halo = (left + right + middle).astype(BF16)
            taps.append(jnp.concatenate([pieces[time][EDGE : EDGE + block], halo], axis=1))
        return jnp.concatenate(taps, axis=0)

    def project(index, taps):
        return jnp.dot(taps, stem_ref[...], preferred_element_type=F32).astype(BF16)

    def keep_rows(index, tokens):
        key = jnp.dot(tokens, w_key[...], preferred_element_type=F32).astype(BF16)
        value = jnp.dot(tokens, w_value[...], preferred_element_type=F32).astype(BF16)
        for pair in range(pairs):
            part = slice(pair * 128, pair * 128 + 128)
            keys[pair, index] = key[:, part]
            values[pair, index] = value[:, part]

    def project_own():
        tokens = project(0, prepare(chan))
        tokens_own[...] = tokens.reshape(times, block, width)
        query = jnp.dot(tokens, w_query[...], preferred_element_type=F32).astype(BF16)
        query = query * BF16(0.125)
        for pair in range(pairs):
            queries[pair] = query[:, pair * 128 : pair * 128 + 128].reshape(times, block, 128)
        keep_rows(0, tokens)

    def project_rest(indices):
        taps = prepare(numbers[indices[0]])
        for at, index in enumerate(indices):
            tokens = project(index, taps)
            if at + 1 < len(indices):
                taps = prepare(numbers[indices[at + 1]])
            keep_rows(index, tokens)

    def project_or_clear(index):
        pl.when(count > index)(lambda: project_rest([index]))

        @pl.when(count <= index)
        def _():
            for pair in range(pairs):
                keys[pair, index] = jnp.zeros((times * block, 128), BF16)
                values[pair, index] = jnp.zeros((times * block, 128), BF16)

    for move in close[1:] + distant:
        shift(*move, "pass")
    for load in loads[:3]:
        load.wait()
    for move in close:
        shift(*move, "take")
    project_own()
    own_tokens = tokens_own[group].astype(F32)
    sums[chan, group] = jnp.sum(own_tokens, axis=0, keepdims=True)
    if flat:

        @pl.when(count == most)
        def _():
            project_rest([1])

        for move in distant:
            shift(*move, "take")

        @pl.when(count == most)
        def _():
            project_rest(range(2, most))

        @pl.when(count < most)
        def _():
            project_rest(range(1, most - 1))
    else:
        for move in distant:
            shift(*move, "take")
        for index in range(1, most):
            project_or_clear(index)

    biases = []
    for index, number in enumerate(numbers):
        listed = neighbours_ref[chan, 0] == number
        for entry in range(1, neighbours_ref.shape[1]):
            listed = listed | (neighbours_ref[chan, entry] == number)
        listed = listed & (count > index)
        biases.append(jnp.where(listed, 0.0, -jnp.inf).astype(F32))

    batch = heads
    span = batch * block
    half = lax.broadcasted_iota(jnp.int32, (span, 128), 1) < HEAD_SIZE

    ones = jnp.ones((times * block, 128), BF16)
    span = block
    half = lax.broadcasted_iota(jnp.int32, (span, 128), 1) < HEAD_SIZE

    def attend(chunk, held):
        units = [(time, pair) for time in range(heads) for pair in range(pairs)]

        def stack(unit):
            time, pair = unit
            both = queries[pair, chunk * heads + time]
            blank = jnp.zeros_like(both)
            return jnp.concatenate(
                [jnp.where(half, both, blank), jnp.where(half, blank, both)], axis=0
            )

        def score(query, pair, number):
            return lax.dot_general(
                query, keys[pair, number], NT_DIMS, preferred_element_type=F32
            )

        query = stack(units[0])
        ahead = [score(query, units[0][1], number) for number in range(held)]
        for at, (time, pair) in enumerate(units):
            scores, ahead = ahead, []
            tops = [
                jnp.max(scores[number], axis=1, keepdims=True) + biases[number]
                for number in range(held)
            ]
            peak = functools.reduce(jnp.maximum, tops)
            if at + 1 < len(units):
                query = stack(units[at + 1])
            output = None
            for number in range(held):
                if at + 1 < len(units):
                    ahead.append(score(query, units[at + 1][1], number))
                weights = jnp.exp(scores[number] - (peak - biases[number])).astype(BF16)
                value = jnp.concatenate([values[pair, number], ones], axis=1)
                part = jnp.dot(weights, value, preferred_element_type=F32)
                output = part if output is None else output + part
            result = output[:, :128] / output[:, 128:]
            attended[chunk * heads + time, pair] = jnp.where(
                half, result[:span], result[span:]
            ).astype(BF16)

    counts = (most - 1, most) if flat else (most,)
    swaps = []
    for far in range(1, tms + 1):
        chunk = lax.rem(tm + far, tms)
        for held in counts:

            def each(held=held):
                attend(chunk, held)

            if len(counts) == 1:
                each()
            else:
                pl.when(count == held)(each)
        for step in range(0 if far < tms else 1, heads):
            to_head = lax.rem(head + step, heads)
            swaps.append(
                send(
                    attended.at[chunk * heads + to_head],
                    received.at[group],
                    swap_sems,
                    far % tms * heads + step,
                    {"tm": chunk, "head": to_head},
                )
            )
    def exchange(buffer, near, sems):
        copies = []
        for number, (far, step) in enumerate(near):
            copies.append(send(buffer, buffer, sems, number, device(far, step)))
        return copies

    for load in loads[3:]:
        load.wait()
    parts = []
    for pair in range(pairs):
        part = attended[:, pair].reshape(times * block, 128).astype(F32)
        parts.append(jnp.sum(part, axis=0, keepdims=True))
    part = jnp.concatenate(parts, axis=1)
    coarse = part.astype(BF16)
    fine = (part - coarse.astype(F32)).astype(BF16)
    mixed = jnp.dot(
        jnp.concatenate([coarse, fine], axis=0),
        w_out[pl.ds(column, slab), :],
        preferred_element_type=F32,
    )
    sums[chan, group] = sums[chan, group] + mixed[:1] + mixed[1:]
    if flat:
        near = sorted(peers, key=lambda pair: -pair[0])
    else:
        near = [pair for pair in peers if pair[0] == 0]
    totals = exchange(sums.at[chan, group], near, sum_sems)
    received[group] = attended[group]
    for copy in swaps:
        copy.wait_recv()
    merged = jnp.concatenate(
        [received[time, pair] for time in range(times) for pair in range(pairs)], axis=1
    )
    branch = jnp.dot(merged, w_out[...], preferred_element_type=F32)
    encoded_ref[...] = (tokens_own[group].astype(F32) + branch).astype(BF16)
    write = pltpu.make_async_copy(encoded_ref, encoded_hbm, w_sem.at[12])
    write.start()

    seismo = seismo_ref[...]
    unit = seismo / jnp.sqrt(jnp.sum(seismo * seismo, axis=1, keepdims=True) + 1e-06)
    unit_coarse = unit.astype(BF16)
    unit_fine = (unit - unit_coarse.astype(F32)).astype(BF16)
    for move in moves:
        shift(*move, "end")
    for copy in swaps:
        copy.wait_send()
    for copy in totals:
        copy.wait_recv()

    summed = range(chans) if flat else [chan]

    def pool(number):
        pooled = sums[number, 0]
        for time in range(1, times):
            pooled = pooled + sums[number, time]
        return pooled / (times * block)

    pooled = jnp.concatenate([pool(number) for number in summed], axis=0)
    projected = jnp.dot(pooled.astype(BF16), w_pool[...], preferred_element_type=F32)
    every = projected * lax.rsqrt(
        jnp.sum(projected * projected, axis=1, keepdims=True) + 1e-06
    )
    if not flat:
        embeds[chan] = every
        near = [pair for pair in peers if pair[1] == 0]
        for copy in exchange(embeds.at[chan], near, embed_sems):
            copy.wait_recv()
        every = jnp.concatenate([embeds[number] for number in range(chans)], axis=0)
    every_coarse = every.astype(BF16)
    every_fine = (every - every_coarse.astype(F32)).astype(BF16)
    logits = 50.0 * lax.dot_general(
        jnp.concatenate([every_coarse, every_fine, every_coarse], axis=1),
        jnp.concatenate([unit_coarse, unit_coarse, unit_fine], axis=1),
        NT_DIMS,
        preferred_element_type=F32,
    )
    spread = jnp.log(jnp.sum(jnp.exp(logits), axis=0, keepdims=True))
    matches = lax.broadcasted_iota(jnp.int32, logits.shape, 0) == colocated_ref[...]
    label = jnp.sum(jnp.where(matches, logits, 0.0), axis=0, keepdims=True)
    loss_ref[...] = spread - label
    store = pltpu.make_async_copy(loss_ref, loss_hbm, w_sem.at[13])
    store.start()
    write.wait()
    store.wait()
    for copy in started[len(swaps) :]:
        copy.wait_send()


def hand_over(encoded_ref, loss_ref, encoded_out, loss_out):
    encoded_out[...] = encoded_ref[...]
    loss_out[...] = loss_ref[...]


def on_device(
    strain, stem_weight, attn_in, attn_out, pool_weight, neighbours, seismo_embed, colocated
):
    chans, tms, heads = (lax.axis_size(axis) for axis in ("chan", "tm", "head"))
    times = tms * heads
    width = attn_in.shape[0]
    slab = width // times
    pairs = slab // 128
    block = strain.shape[1] // PC
    reach = 2 if chans <= 4 else 3
    own = reach + 1
    gathered = 2 * own + 1
    most = min(2 * reach + 1, chans)
    place, pick = tap_tables()
    vmem = pl.BlockSpec(memory_space=pltpu.VMEM)
    hbm = pl.BlockSpec(memory_space=pl.ANY)
    dma = pltpu.SemaphoreType.DMA
    sizes = (chans, tms, heads, block, slab, width, own, most)
    shapes = (
        jax.ShapeDtypeStruct((block, width), BF16),
        jax.ShapeDtypeStruct((1, seismo_embed.shape[0]), F32),
    )
    encoded, loss = pl.pallas_call(
        functools.partial(layer, sizes),
        out_shape=shapes,
        in_specs=[hbm] * 10,
        out_specs=(hbm, hbm),
        scratch_shapes=[
            pltpu.VMEM((times, gathered, block, 128), BF16),
            pltpu.VMEM((times, block, width), BF16),
            pltpu.VMEM((pairs, times, block, 128), BF16),
            pltpu.VMEM((pairs, most, times * block, 128), BF16),
            pltpu.VMEM((pairs, most, times * block, 128), BF16),
            pltpu.VMEM((times, pairs, block, 128), BF16),
            pltpu.VMEM((times, pairs, block, 128), BF16),
            pltpu.VMEM((chans, times, 1, width), F32),
            pltpu.VMEM((chans, 1, pool_weight.shape[1]), F32),
            pltpu.VMEM((width, slab), BF16),
            pltpu.VMEM((width, slab), BF16),
            pltpu.VMEM((width, slab), BF16),
            pltpu.VMEM(attn_out.shape, BF16),
            pltpu.VMEM(pool_weight.shape, BF16),
            pltpu.VMEM(strain.shape, BF16),
            pltpu.VMEM(stem_weight.shape, BF16),
            pltpu.VMEM((256, width), BF16),
            pltpu.VMEM(place.shape, BF16),
            pltpu.VMEM(pick.shape, BF16),
            pltpu.VMEM(seismo_embed.shape, F32),
            pltpu.VMEM((1, seismo_embed.shape[0]), jnp.int32),
            pltpu.VMEM((block, width), BF16),
            pltpu.VMEM((1, seismo_embed.shape[0]), F32),
            pltpu.SMEM(neighbours.shape, jnp.int32),
            dma((14,)),
            pltpu.SemaphoreType.REGULAR((2, chans)),
            dma((2, tms * gathered)),
            dma((2, tms * gathered * heads)),
            dma((2, times)),
            dma((2, chans * times)),
            dma((2, chans)),
        ],
        compiler_params=pltpu.CompilerParams(
            collective_id=0, has_side_effects=True, vmem_limit_bytes=56 * 1024 * 1024
        ),
    )(
        strain,
        stem_weight,
        attn_in,
        attn_out,
        pool_weight,
        jnp.asarray(place, BF16),
        jnp.asarray(pick, BF16),
        neighbours,
        seismo_embed,
        colocated[None, :],
    )
    encoded, loss = pl.pallas_call(
        hand_over,
        out_shape=shapes,
        in_specs=[vmem, vmem],
        out_specs=(vmem, vmem),
    )(encoded, loss)
    return (encoded[None], loss[0])


def solution(mesh):
    in_specs = (
        P(("grp", "tm", "head"), "chan"),
        P(),
        P(),
        P(),
        P(),
        P("grp", None),
        P("grp", None),
        P("grp"),
    )
    out_specs = (P(("grp", "tm", "head"), "chan", None), P("grp"))
    return jax.shard_map(
        on_device, mesh=mesh, in_specs=in_specs, out_specs=out_specs, check_vma=False
    )
```
